32 devices in a mesh: groups: 1, seq: 32 (over z, y, x, core).
Axes of the slice: x: 2, y: 2, z: 4, core: 2. Of those that a mesh axis runs over, the one named last changes fastest.
Arguments:
- video_heads: bfloat16 [16, 4, 1024, 384], P('groups', None, 'seq'), may hold values from -60 to 60
- image_heads: bfloat16 [16, 4, 512, 256], P('groups', None, 'seq'), may hold values from -6 to 6
- audio_queries: bfloat16 [2, 1024, 2048], P('groups', 'seq'), may hold values from -60 to 60
- audio_keys: bfloat16 [64, 4096], P('seq', 'groups'), may hold values from -8 to 8
- condition_flags: int32 [2, 4], P('groups'), may hold values from 0 to 1, as said below
- guidance_weights: int32 [4], P('groups'), may hold values from -8 to 24
- token_frame: int32 [1024], P('groups'), may hold values from 0 to 15, never falling along the last dimension, each value on 1 to 128 neighbouring positions
- window_start: int32 [16], P('groups'), may hold values from 0 to 32
- modulation: float32 [2, 4, 2048], P('groups'), may hold values from -3 to 3
- final_weight: bfloat16 [2048, 64], replicated, may hold values from -0.125 to 0.125
- noisy_latent: float32 [1024, 64], P(('groups', 'seq')), may hold values from -6 to 6
Outputs:
- velocity: float32 [1024, 64], P(('groups', 'seq'))
- next_latent: float32 [1024, 64], P(('groups', 'seq'))
The draws below stay inside these ranges and needn't reach their ends.
Inputs may be any that keep to these rules, and one draw needn't show every extreme that they name: `condition_flags`: each of the four pairs (audio flag, image flag) occurs in exactly one branch.
All inputs are finite; a program needn't handle non-finite values.
Results may differ from the reference program's by a relative error of at most 0.0045.
Values may be sent and summed in bfloat16 or wider, within the bound.
A program may use at most 64 MiB of HBM per device.

```python
import math
import jax
import jax.numpy as jnp
import numpy as np
from jax import lax

HEADS = 16
HEAD_DIM = 128
CH = 64
BRANCHES = 4
AUD_WIN = 32
FRAMES = 16
TOKENS = 1024
IMG = 512
AUDIO = 64
INNER = 2048
AUDIO_BR = 2


def draw_condition_flags(key, part):
    order = jax.random.permutation(key, BRANCHES).astype(jnp.int32)
    return jnp.stack([order % 2, order // 2]).astype(jnp.int32)


def draw_video_heads(key, part):
    full_shape = (HEADS, BRANCHES, TOKENS, 3 * HEAD_DIM)
    values = jax.random.truncated_normal(key, -6.0, 6.0, full_shape, jnp.float32)
    return values.astype(jnp.bfloat16)


def audio_pair(key):
    query_key = jax.random.fold_in(key, 101)
    pair_key = jax.random.fold_in(key, 202)
    query_shape = (AUDIO_BR, TOKENS, INNER)
    pair_shape = (AUDIO, 2 * INNER)
    pairs = jax.random.truncated_normal(pair_key, -6.0, 6.0, pair_shape, jnp.float32)
    keys_part = pairs[:, :INNER]
    values_part = 0.1 * pairs[:, INNER:]
    queries = jax.random.truncated_normal(query_key, -6.0, 6.0, query_shape, jnp.float32)
    return (queries, jnp.concatenate([keys_part, values_part], axis=1))


def draw_audio_queries(key, part):
    queries, pairs = audio_pair(key)
    return queries.astype(jnp.bfloat16)


def draw_audio_keys(key, part):
    queries, pairs = audio_pair(key)
    return pairs.astype(jnp.bfloat16)


def with_ends(values, key, least, high):
    place = [jax.random.randint(jax.random.fold_in(key, axis), (), 0, length) for axis, length in enumerate(values.shape)]
    widest = values.shape.index(max(values.shape))
    next_to = place[:widest] + [(place[widest] + 1) % values.shape[widest]] + place[widest + 1:]
    return values.at[tuple(place)].set(least).at[tuple(next_to)].set(high)


def block_levels(key, extent, shards, least, largest):
    factor_of = 1.0
    for dim, parts in shards:
        steps = jax.random.uniform(jax.random.fold_in(jax.random.fold_in(key, 6), dim), (parts,), jnp.float32, least / len(shards), largest / len(shards))
        factor_of = factor_of * jnp.repeat(jnp.exp(steps), extent[dim] // parts).reshape((-1,) + (1,) * (len(extent) - 1 - dim))
    return factor_of


def length_profile(count, total, bound, slope):
    portions = [(1 << 20) // math.isqrt(grade ** slope) + 1 for grade in range(2, count + 1)]
    rest, counts = total - bound - (count - 1), [1] * (count - 1)
    while rest > 0:
        candidates = [i for i in range(count - 1) if counts[i] < bound]
        whole, remaining = sum([portions[i] for i in candidates]), rest
        for i in candidates:
            addition = min(bound - counts[i], max(1, remaining * portions[i] // whole), rest)
            counts[i] = counts[i] + addition
            rest = rest - addition
    return np.array([bound] + counts)


def ragged(stream_key, amount, total, most, lean):
    if amount == 2:
        one = jax.random.randint(stream_key, (), max(1, total - most), min(most, total - 1) + 1)
        return jnp.stack([one, total - one])
    tallies = jnp.asarray(length_profile(amount, total, most, lean), jnp.int32)
    pairs = (amount - 1) // 2
    source_of, taker = tallies[1:1 + 2 * pairs:2], tallies[2:2 + 2 * pairs:2]
    room = jnp.minimum(source_of - 1, most - taker)
    passed = jax.random.randint(jax.random.fold_in(stream_key, 1), (pairs,), 0, 1 << 20) % (room + 1)
    tallies = tallies.at[1:1 + 2 * pairs:2].set(source_of - passed).at[2:2 + 2 * pairs:2].set(taker + passed)
    return tallies[jax.random.permutation(jax.random.fold_in(stream_key, 2), amount)]


def bell_draw(rng, dims, deviation, bound, shards=(), kind=jnp.bfloat16):
    entries = jax.random.normal(rng, dims, jnp.float32) * deviation
    if len(shards) > 0:
        entries = block_levels(rng, dims, shards, -0.22, 0.18) * entries
    return jnp.clip(entries, min=-bound, max=bound).astype(kind)


def setup_inputs(seed: int = 0, part: int = 0) -> dict:
    splits = jax.random.split(jax.random.key(seed), 12)
    part_splits = jax.random.split(jax.random.fold_in(splits[11], part), 12)
    return {
        "video_heads": draw_video_heads(jax.random.fold_in(jax.random.fold_in(splits[11], part), 71), part),
        "image_heads": bell_draw(part_splits[1], (HEADS, BRANCHES, IMG, 2 * HEAD_DIM), 1.0, 6.0, ((2, 32),)),
        "audio_queries": draw_audio_queries(jax.random.fold_in(jax.random.fold_in(splits[11], part), 71), part),
        "audio_keys": draw_audio_keys(jax.random.fold_in(jax.random.fold_in(splits[11], part), 71), part),
        "condition_flags": draw_condition_flags(jax.random.fold_in(jax.random.fold_in(splits[11], part), 71), part),
        "guidance_weights": with_ends(jax.random.randint(part_splits[5], (BRANCHES,), -8, 25), jax.random.fold_in(part_splits[5], 1), -8, 24).astype(jnp.int32),
        "token_frame": jnp.searchsorted(jnp.cumsum(ragged(part_splits[6], FRAMES, TOKENS, 2 * TOKENS // FRAMES, 0)), jnp.arange(TOKENS), side="right").astype(jnp.int32),
        "window_start": with_ends(jax.random.randint(part_splits[7], (FRAMES,), 0, AUDIO - AUD_WIN + 1), jax.random.fold_in(part_splits[7], 1), 0, AUDIO - AUD_WIN).astype(jnp.int32),
        "modulation": bell_draw(part_splits[8], (2, BRANCHES, INNER), 0.5, 3.0, (), jnp.float32),
        "final_weight": bell_draw(splits[9], (INNER, CH), INNER ** -0.5, 0.125),
        "noisy_latent": bell_draw(part_splits[10], (TOKENS, CH), 1.0, 6.0, ((0, 32),), jnp.float32),
    }


def attend_rows(queries, video_pairs, image_pairs, image_mark):
    rows, head_dim = queries.shape
    score_scale = 1.0 / math.sqrt(head_dim)
    block_size = min(512, rows)
    video_keys = video_pairs[:, :head_dim]
    video_values = video_pairs[:, head_dim:]
    image_keys = image_pairs[:, :head_dim]
    image_values = image_pairs[:, head_dim:]

    def with_image(query_block):
        video_scores = jnp.dot(query_block, video_keys.T, preferred_element_type=jnp.float32) * score_scale
        image_scores = jnp.dot(query_block, image_keys.T, preferred_element_type=jnp.float32) * score_scale
        row_top = jnp.maximum(lax.optimization_barrier(jnp.max(video_scores, axis=1, keepdims=True)), lax.optimization_barrier(jnp.max(image_scores, axis=1, keepdims=True)))
        video_weights = jnp.exp(video_scores - row_top)
        image_weights = jnp.exp(image_scores - row_top)
        row_total = lax.optimization_barrier(jnp.sum(video_weights, axis=1, keepdims=True)) + lax.optimization_barrier(jnp.sum(image_weights, axis=1, keepdims=True))
        blended = jnp.dot(video_weights.astype(jnp.bfloat16), video_values, preferred_element_type=jnp.float32)
        blended = blended + jnp.dot(image_weights.astype(jnp.bfloat16), image_values, preferred_element_type=jnp.float32)
        return (blended / row_total).astype(jnp.bfloat16)

    def without_image(query_block):
        video_scores = jnp.dot(query_block, video_keys.T, preferred_element_type=jnp.float32) * score_scale
        row_top = lax.optimization_barrier(jnp.max(video_scores, axis=1, keepdims=True))
        video_weights = jnp.exp(video_scores - row_top)
        row_total = lax.optimization_barrier(jnp.sum(video_weights, axis=1, keepdims=True))
        blended = jnp.dot(video_weights.astype(jnp.bfloat16), video_values, preferred_element_type=jnp.float32)
        return (blended / row_total).astype(jnp.bfloat16)

    def one_block(query_block):
        return lax.cond(image_mark > 0, with_image, without_image, query_block)
    blocks = queries.reshape(rows // block_size, block_size, head_dim)
    return lax.map(one_block, blocks).reshape(rows, head_dim)

def window_mask(frames_here, window_start, audio_count):
    frame_ids = jnp.arange(window_start.shape[0], dtype=jnp.int32)
    matches = frames_here[:, None] == frame_ids[None, :]
    starts = lax.optimization_barrier(jnp.sum(jnp.where(matches, window_start[None, :], 0), axis=1))
    positions = jnp.arange(audio_count, dtype=jnp.int32)
    return (positions[None, :] >= starts[:, None]) & (positions[None, :] < starts[:, None] + AUD_WIN)

def audio_attention(queries, audio_pairs, inside, heads):
    audio_branches, rows, inner = queries.shape
    head_dim = inner // heads
    score_scale = 1.0 / math.sqrt(head_dim)
    split_queries = queries.reshape(audio_branches, rows, heads, head_dim).astype(jnp.float32)
    audio_count = audio_pairs.shape[0]
    keys_part = audio_pairs[:, :inner].reshape(audio_count, heads, head_dim).astype(jnp.float32)
    values_part = audio_pairs[:, inner:].reshape(audio_count, heads, head_dim)
    scores = jnp.einsum('brhd,nhd->bhrn', split_queries, keys_part) * score_scale
    scores = jnp.where(inside[None, None], scores, -jnp.inf)
    row_top = lax.optimization_barrier(jnp.max(scores, axis=3, keepdims=True))
    weights = jnp.where(inside[None, None], jnp.exp(scores - row_top), 0.0)
    row_total = lax.optimization_barrier(jnp.sum(weights, axis=3, keepdims=True))
    rounded = weights.astype(jnp.bfloat16).astype(jnp.float32)
    blended = jnp.einsum('bhrn,nhd->bhrd', rounded, values_part.astype(jnp.float32)) / row_total
    return blended.transpose(0, 2, 1, 3).reshape(audio_branches, rows, inner)

def finish(attention, audio_out, condition_flags, guidance_weights, modulation, final_weight, noisy_latent):
    branches, rows, inner = attention.shape
    audio_mark = condition_flags[0]
    ranks = jnp.cumsum(audio_mark) - 1
    select = ((audio_mark[:, None] == 1) & (ranks[:, None] == jnp.arange(2, dtype=jnp.int32)[None, :])).astype(jnp.float32)
    added = lax.optimization_barrier(jnp.sum(select[:, :, None, None] * audio_out[None], axis=1))
    hidden = attention.astype(jnp.float32) + added
    center = lax.optimization_barrier(jnp.mean(hidden, axis=2, keepdims=True))
    spread = lax.optimization_barrier(jnp.mean(jnp.square(hidden - center), axis=2, keepdims=True))
    normed = (hidden - center) * lax.rsqrt(spread + 1e-06)
    modulated = (normed * (1.0 + modulation[1][:, None, :]) + modulation[0][:, None, :]).astype(jnp.bfloat16)
    branch_velocity = jnp.dot(modulated.reshape(branches * rows, inner), final_weight, preferred_element_type=jnp.float32)
    branch_velocity = branch_velocity.reshape(branches, rows, final_weight.shape[1])
    mixing = guidance_weights.astype(jnp.float32) / 8.0
    velocity = lax.optimization_barrier(jnp.sum(mixing[:, None, None] * branch_velocity, axis=0))
    return (velocity, noisy_latent - 0.125 * velocity)

def reference(video_heads, image_heads, audio_queries, audio_keys, condition_flags, guidance_weights, token_frame, window_start, modulation, final_weight, noisy_latent):
    heads, branches, tokens, width_three = video_heads.shape
    head_dim = width_three // 3
    image_rows = image_heads.shape[2]
    video_items = video_heads.reshape(heads * branches, tokens, width_three)
    image_items = image_heads.reshape(heads * branches, image_rows, 2 * head_dim)
    branch_of = jnp.arange(heads * branches, dtype=jnp.int32) % branches
    marks = condition_flags[1][branch_of]

    def one_item(packed):
        video_item, image_item, image_mark = packed
        return attend_rows(video_item[:, :head_dim], video_item[:, head_dim:], image_item, image_mark)
    outputs = lax.map(one_item, (video_items, image_items, marks))
    attention = outputs.reshape(heads, branches, tokens, head_dim).transpose(1, 2, 0, 3).reshape(branches, tokens, heads * head_dim)
    inside = window_mask(token_frame, window_start, audio_keys.shape[0])
    audio_out = audio_attention(audio_queries, audio_keys, inside, heads)
    return finish(attention, audio_out, condition_flags, guidance_weights, modulation, final_weight, noisy_latent)
```

```python
import functools
import math

import jax
import jax.numpy as jnp
from jax import lax
from jax.experimental import pallas as pl
from jax.experimental.pallas import tpu as pltpu
from jax.sharding import PartitionSpec as P

AUD_WIN = 32
PAIRS = ((1, 1), (1, 0), (0, 1), (0, 0))


def step_kernel(
    n,
    q_block,
    plane,
    flags_in,
    guide_in,
    frames_in,
    starts_in,
    video_in,
    image_in,
    audio_q_in,
    audio_kv_in,
    modulation_in,
    final_weight_in,
    mixed,
    flags,
    guide,
    frames,
    starts,
    video,
    image,
    audio_q,
    audio_kv,
    modulation,
    final_weight,
    loads,
    staged,
    staged_img,
    got,
    got_img,
    outs,
    back,
    gathered,
    audio_wide,
    audio_out,
    hidden,
    send_v,
    recv_v,
    send_i,
    recv_i,
    send_a,
    recv_a,
    send_b,
    recv_b,
    send_o,
    recv_o,
):
    heads, branches, rows, wide = video.shape
    dim = wide // 3
    img_rows = image.shape[2]
    inner = heads * dim
    units = heads * branches // n
    tokens = n * rows
    me = lax.axis_index("seq")
    bits = (n - 1).bit_length()
    flips = [(1 - 2 * ((me // 2**i) % 2)) * 2**i for i in range(bits)]

    def partner(k):
        other = me
        for i in range(bits):
            other = other + ((k // 2**i) % 2) * flips[i]
        return other

    def each_peer(body):
        def step(i, carry):
            body(partner(n - 1 - i))
            return carry

        lax.fori_loop(0, n - 1, step, 0)

    def send(src, dst, s_sem, r_sem, other):
        pltpu.make_async_remote_copy(
            src_ref=src,
            dst_ref=dst,
            send_sem=s_sem,
            recv_sem=r_sem,
            device_id={"seq": other},
            device_id_type=pl.DeviceIdType.MESH,
        ).start()

    def drain(ref, sem):
        pltpu.make_async_copy(ref, ref, sem).wait()

    pairs = (
        (flags_in, flags),
        (video_in, video),
        (image_in, image),
        (audio_kv_in, audio_kv),
        (frames_in, frames),
        (starts_in, starts),
        (guide_in, guide),
        (audio_q_in, audio_q),
        (modulation_in, modulation),
        (final_weight_in, final_weight),
    )
    fetches = [pltpu.make_async_copy(src, dst, loads.at[i]) for i, (src, dst) in enumerate(pairs)]
    for fetch in fetches:
        fetch.start()

    barrier = pltpu.get_barrier_semaphore()
    each_peer(
        lambda other: pl.semaphore_signal(
            barrier, inc=1, device_id={"seq": other}, device_id_type=pl.DeviceIdType.MESH
        )
    )

    for fetch in fetches[:4]:
        fetch.wait()
    place = []
    for aud, img in PAIRS:
        at = jnp.int32(0)
        for b in range(branches):
            f0, f1 = flags[0, b], flags[1, b]
            at = at + b * ((f0 if aud else 1 - f0) * (f1 if img else 1 - f1))
        place.append(jnp.minimum(at, branches - 1))

    def stage(h, carry):
        for p in range(branches):
            staged[h * branches + p] = video[h, place[p]]
        for p in range(0, branches, 2):
            staged_img[h * (branches // 2) + p // 2] = image[h, place[p]]
        return carry

    lax.fori_loop(0, heads, stage, 0)
    pl.semaphore_wait(barrier, n - 1)

    mine = pl.ds(pl.multiple_of(me * rows, rows), rows)
    mine_img = pl.ds(pl.multiple_of(me * img_rows, img_rows), img_rows)

    strips = n // plane
    my_strip, my_seat = me // plane, me % plane
    pltpu.sync_copy(audio_kv, gathered.at[my_seat, my_strip])

    def far(i, carry):
        strip = (my_strip + 1 + i) % strips
        send(
            audio_kv,
            gathered.at[my_seat, my_strip],
            send_a,
            recv_a,
            strip * plane + my_seat,
        )
        return carry

    lax.fori_loop(0, strips - 1, far, 0)

    def send_unit(j):
        each_peer(
            lambda other: send(
                staged.at[other * units + j], got.at[j, mine], send_v.at[j], recv_v.at[j], other
            )
        )

    def send_image(m):
        def one(other):
            if units > 1:
                item = other * (units // 2) + m
                send(staged_img.at[item], got_img.at[m, mine_img], send_i.at[m], recv_i.at[m], other)
            else:

                @pl.when(other % 2 == 0)
                def _():
                    send(
                        staged_img.at[other // 2],
                        got_img.at[m, mine_img],
                        send_i.at[m],
                        recv_i.at[m],
                        other,
                    )

        each_peer(one)

    send_unit(0)
    send_image(0)
    drain(gathered.at[0, pl.ds(0, strips - 1)], recv_a)

    def near(i, carry):
        seat = (my_seat + 1 + i) % plane
        send(
            gathered.at[my_seat], gathered.at[my_seat], send_b, recv_b, my_strip * plane + seat
        )
        return carry

    lax.fori_loop(0, plane - 1, near, 0)
    for j in range(1, units):
        send_unit(j)
        if j % 2 == 0:
            send_image(j // 2)

    for j in range(units):
        got[j, mine] = staged[me * units + j]
    if units > 1:
        for m in range(units // 2):
            got_img[m, mine_img] = staged_img[me * (units // 2) + m]
    else:

        @pl.when(me % 2 == 0)
        def _():
            got_img[0, mine_img] = staged_img[me // 2]

    for fetch in fetches[4:]:
        fetch.wait()
    spots = lax.broadcasted_iota(jnp.int32, (rows, 1), 0)

    def start_of(t, column):
        return jnp.where(spots == t, starts[frames[me * rows + t]], column)

    first = lax.fori_loop(0, rows, start_of, jnp.zeros((rows, 1), jnp.int32))
    audio_rows = audio_kv.shape[0]
    audio_count = n * audio_rows
    slots = lax.broadcasted_iota(jnp.int32, (rows, audio_count), 1)
    inside = (slots >= first) & (slots < first + AUD_WIN)
    ranks = audio_q.shape[0]
    inside = jnp.concatenate([inside] * ranks, axis=0)

    drain(gathered.at[pl.ds(0, plane - 1)], recv_b)
    per = 8 // audio_rows

    def widen(g, carry):
        pieces = []
        for i in range(per):
            src = g * per + i
            pieces.append(gathered[src % plane, src // plane].astype(jnp.float32))
        audio_wide[pl.ds(pl.multiple_of(g * 8, 8), 8), :] = jnp.concatenate(pieces, axis=0)
        return carry

    lax.fori_loop(0, audio_count // 8, widen, 0)
    scale = 1.0 / math.sqrt(dim)
    log2e = math.log2(math.e)
    transposed = (((1,), (1,)), ((), ()))

    def audio_head(h, carry):
        cols = pl.ds(pl.multiple_of(h * dim, dim), dim)
        val_cols = pl.ds(pl.multiple_of(inner + h * dim, dim), dim)
        q = audio_q[:, :, cols].reshape(ranks * rows, dim)
        k = audio_wide[:, cols].astype(jnp.bfloat16)
        v = audio_wide[:, val_cols].astype(jnp.bfloat16)
        s = lax.dot_general(q, k, transposed, preferred_element_type=jnp.float32)
        s = jnp.where(inside, s, -jnp.inf)
        top = jnp.max(s, axis=1, keepdims=True)
        w = jnp.where(inside, jnp.exp2((s - top) * (scale * log2e)), 0.0)
        total = jnp.sum(w, axis=1, keepdims=True)
        o = jnp.dot(w.astype(jnp.bfloat16), v, preferred_element_type=jnp.float32) / total
        audio_out[:, :, cols] = o.reshape(ranks, rows, dim)
        return carry

    lax.fori_loop(0, heads, audio_head, 0)

    blocks = tokens // q_block
    per_block = q_block // rows
    turn = me // per_block + 1

    def attend(j, with_image):
        def block(i, carry):
            b = (turn + i) % blocks
            at = pl.ds(pl.multiple_of(b * q_block, q_block), q_block)
            q = got[j, at, 0:dim]
            k = got[j, :, dim : 2 * dim]
            v = got[j, :, 2 * dim :]
            s = lax.dot_general(q, k, transposed, preferred_element_type=jnp.float32)
            top = jnp.max(s, axis=1, keepdims=True)
            if with_image:
                ki = got_img[j // 2, :, 0:dim]
                vi = got_img[j // 2, :, dim:]
                si = lax.dot_general(q, ki, transposed, preferred_element_type=jnp.float32)
                top = jnp.maximum(top, jnp.max(si, axis=1, keepdims=True))
            w = jnp.exp2((s - top) * (scale * log2e))
            total = jnp.sum(w, axis=1, keepdims=True)
            o = jnp.dot(w.astype(jnp.bfloat16), v, preferred_element_type=jnp.float32)
            if with_image:
                wi = jnp.exp2((si - top) * (scale * log2e))
                total = total + jnp.sum(wi, axis=1, keepdims=True)
                o = o + jnp.dot(wi.astype(jnp.bfloat16), vi, preferred_element_type=jnp.float32)
            outs[j, at, :] = (o / total).astype(jnp.bfloat16)

            def give(d, inner_carry):
                other = b * per_block + d
                part = outs.at[j, pl.ds(pl.multiple_of(other * rows, rows), rows)]

                @pl.when(other != me)
                def _():
                    send(part, back.at[j, me], send_o.at[j], recv_o.at[j], other)

                return inner_carry

            lax.fori_loop(0, per_block, give, 0)
            return carry

        lax.fori_loop(0, blocks, block, 0)
        back[j, me] = outs[j, mine, :]

    for j in range(units):
        drain(got.at[j, pl.ds(0, (n - 1) * rows)], recv_v.at[j])
        if units > 1:
            if j % 2 == 0:
                drain(got_img.at[j // 2, pl.ds(0, (n - 1) * img_rows)], recv_i.at[j // 2])
            attend(j, j % 2 == 0)
        else:

            @pl.when(me % 2 == 0)
            def _():
                drain(got_img.at[0, pl.ds(0, (n - 1) * img_rows)], recv_i.at[0])
                attend(0, True)

            @pl.when(me % 2 == 1)
            def _():
                attend(0, False)

    swapped = jnp.where(place[0] > place[1], 1, 0)
    seats = (swapped, 1 - swapped)
    result = jnp.zeros(mixed.shape, jnp.float32)
    for j in range(units):
        drain(back.at[j, pl.ds(0, n - 1)], recv_o.at[j])
        for p in range(j, branches, units):
            for h in range(heads):
                cols = slice(h * dim, (h + 1) * dim)
                x = back[j, (h * branches + p) // units].astype(jnp.float32)
                if PAIRS[p][0]:
                    x = x + audio_out[seats[p], :, cols]
                hidden[:, cols] = x
            x = hidden[...]
            center = jnp.mean(x, axis=1, keepdims=True)
            x = x - center
            spread = jnp.mean(jnp.square(x), axis=1, keepdims=True)
            x = x * lax.rsqrt(spread + 1e-06)
            gain = modulation[1, pl.ds(place[p], 1), :]
            shift = modulation[0, pl.ds(place[p], 1), :]
            x = (x * (1.0 + gain) + shift).astype(jnp.bfloat16)
            y = lax.dot_general(x, final_weight[...], transposed, preferred_element_type=jnp.float32)
            result = result + guide[place[p]].astype(jnp.float32) * y
    mixed[...] = result

    drain(gathered.at[0, pl.ds(0, strips - 1)], send_a)
    drain(gathered.at[pl.ds(0, plane - 1)], send_b)
    for j in range(units):
        drain(staged.at[pl.ds(0, n - 1)], send_v.at[j])
        drain(back.at[j, pl.ds(0, n - 1)], send_o.at[j])
    if units > 1:
        for m in range(units // 2):
            drain(staged_img.at[pl.ds(0, n - 1)], send_i.at[m])
    else:

        @pl.when(me % 2 == 0)
        def _():
            drain(staged_img.at[pl.ds(0, n // 2 - 1)], send_i.at[0])

        @pl.when(me % 2 == 1)
        def _():
            drain(staged_img.at[pl.ds(0, n // 2)], send_i.at[0])


def split_kernel(
    n,
    q_block,
    plane,
    flags_in,
    guide_in,
    frames_in,
    starts_in,
    video_in,
    image_in,
    audio_q_in,
    audio_kv_in,
    modulation_in,
    final_weight_in,
    mixed,
    flags,
    guide,
    frames,
    starts,
    video,
    image,
    audio_q,
    audio_kv,
    modulation,
    final_weight,
    loads,
    st_q,
    st_k,
    st_c,
    got_q,
    got_k,
    got_c,
    out_b,
    out_s,
    out_c,
    back_b,
    back_s,
    back_c,
    gathered,
    audio_wide,
    audio_out,
    hidden,
    weights,
    sends,
    recvs,
):
    heads, branches, rows, wide = video.shape
    dim = wide // 3
    img_rows = image.shape[2]
    inner = heads * dim
    half = n // 2
    me = lax.axis_index("seq")
    loc = me % half
    bits = (n - 1).bit_length()
    flips = [(1 - 2 * ((me // 2**i) % 2)) * 2**i for i in range(bits)]

    def partner(k):
        other = me
        for i in range(bits):
            other = other + ((k // 2**i) % 2) * flips[i]
        return other

    def loop(count, body):
        def step(i, carry):
            body(i)
            return carry

        lax.fori_loop(0, count, step, 0)

    def send(src, dst, which, other):
        pltpu.make_async_remote_copy(
            src_ref=src,
            dst_ref=dst,
            send_sem=sends.at[which],
            recv_sem=recvs.at[which],
            device_id={"seq": other},
            device_id_type=pl.DeviceIdType.MESH,
        ).start()

    def drain(ref, sem):
        pltpu.make_async_copy(ref, ref, sem).wait()

    Q, K, C, FAR, NEAR, RB, RS, RC = range(8)

    barrier = pltpu.get_barrier_semaphore()
    loop(
        n - 1,
        lambda i: pl.semaphore_signal(
            barrier, inc=1, device_id={"seq": partner(n - 1 - i)}, device_id_type=pl.DeviceIdType.MESH
        ),
    )
    pairs = (
        (flags_in, flags),
        (video_in, video),
        (image_in, image),
        (audio_kv_in, audio_kv),
        (frames_in, frames),
        (starts_in, starts),
        (guide_in, guide),
        (audio_q_in, audio_q),
        (modulation_in, modulation),
        (final_weight_in, final_weight),
    )
    fetches = [pltpu.make_async_copy(src, dst, loads.at[i]) for i, (src, dst) in enumerate(pairs)]
    for fetch in fetches:
        fetch.start()
    for fetch in fetches[:4]:
        fetch.wait()
    place = []
    for aud, img in PAIRS:
        at = jnp.int32(0)
        for b in range(branches):
            f0, f1 = flags[0, b], flags[1, b]
            at = at + b * ((f0 if aud else 1 - f0) * (f1 if img else 1 - f1))
        place.append(jnp.minimum(at, branches - 1))

    def stage(h):
        for j in range(2):
            x = video[h, place[2 * j]]
            st_q[h, :, j * dim : (j + 1) * dim] = x[:, :dim]
            st_k[h, :, 2 * j * dim : 2 * (j + 1) * dim] = x[:, dim:]
            st_k[h, j * img_rows : (j + 1) * img_rows, 4 * dim :] = image[h, place[2 * j]]
            st_c[2 * h + j] = video[h, place[2 * j + 1]]

    loop(heads, stage)
    pl.semaphore_wait(barrier, n - 1)

    strips = n // plane
    my_strip, my_seat = me // plane, me % plane
    pltpu.sync_copy(audio_kv, gathered.at[my_seat, my_strip])

    def far(i):
        strip = (my_strip + 1 + i) % strips
        send(audio_kv, gathered.at[my_seat, my_strip], FAR, strip * plane + my_seat)

    loop(strips - 1, far)

    def send_q(other):
        send(st_q.at[other % half], got_q.at[me], Q, other)

    def send_k(other):
        send(st_k.at[other % half], got_k.at[loc], K, other)

    def send_c(other):
        send(st_c.at[other], got_c.at[me], C, other)

    def first(i):
        send_q(partner(n - 1 - i))

        @pl.when(i < half - 1)
        def _():
            other = partner(half - 1 - i)
            send_k(other)
            send_q(other)

    loop(half, first)
    drain(gathered.at[0, pl.ds(0, strips - 1)], recvs.at[FAR])

    def near(i):
        seat = (my_seat + 1 + i) % plane
        send(gathered.at[my_seat], gathered.at[my_seat], NEAR, my_strip * plane + seat)

    loop(plane - 1, near)

    def second(i):
        send_c(partner(n - 1 - i))

        @pl.when(i < half - 1)
        def _():
            send_c(partner(half - 1 - i))

    loop(half, second)

    got_q[me] = st_q[loc]
    got_k[loc] = st_k[loc]
    got_c[me] = st_c[me]

    scale = 1.0 / math.sqrt(dim)
    rate = scale * math.log2(math.e)
    transposed = (((1,), (1,)), ((), ()))

    blocks = n * rows // q_block
    per_block = q_block // rows
    turn = me // per_block + 1

    def attend(q, keys, values):
        scores = [lax.dot_general(q, k, transposed, preferred_element_type=jnp.float32) for k in keys]
        top = functools.reduce(jnp.maximum, [jnp.max(s, axis=1, keepdims=True) for s in scores])
        total, o = 0.0, 0.0
        for s, v in zip(scores, values):
            w = jnp.exp2((s - top) * rate)
            total = total + jnp.sum(w, axis=1, keepdims=True)
            o = o + jnp.dot(w.astype(jnp.bfloat16), v, preferred_element_type=jnp.float32)
        return (o / total).astype(jnp.bfloat16), top, total

    def give(b, body):
        def one(d):
            other = b * per_block + d

            @pl.when(other != me)
            def _():
                body(other)

        loop(per_block, one)

    drain(got_q.at[pl.ds(0, n - 1)], recvs.at[Q])
    drain(got_k.at[pl.ds(0, half - 1)], recvs.at[K])

    lane = lax.broadcasted_iota(jnp.int32, (q_block, 4 * rows), 1)
    diagonal = lane % rows == lax.broadcasted_iota(jnp.int32, (q_block, 4 * rows), 0) % rows

    def image_block(i):
        b = (turn + i) % blocks
        devices = pl.ds(pl.multiple_of(b * per_block, per_block), per_block)
        stats = []
        for j in range(2):
            q = got_q[devices, :, j * dim : (j + 1) * dim].reshape(q_block, dim)
            at = 2 * j * dim
            k = got_k[:, :, at : at + dim].reshape(half * rows, dim)
            v = got_k[:, :, at + dim : at + 2 * dim].reshape(half * rows, dim)
            pick = slice(j * img_rows, (j + 1) * img_rows)
            ki = got_k[:, pick, 4 * dim : 5 * dim].reshape(half * img_rows, dim)
            vi = got_k[:, pick, 5 * dim :].reshape(half * img_rows, dim)
            o, top, total = attend(q, (k, ki), (v, vi))
            out_b[devices, :, j * dim : (j + 1) * dim] = o.reshape(per_block, rows, dim)
            stats += [top, total]
        x = jnp.where(lane < rows, stats[0], jnp.where(lane < 2 * rows, stats[1], jnp.where(lane < 3 * rows, stats[2], stats[3])))
        x = jnp.where(diagonal, x, 0.0).reshape(per_block, rows, 4 * rows)
        out_s[devices, 0, :] = jnp.sum(x, axis=1)

        def body(other):
            send(out_b.at[other], back_b.at[me], RB, other)
            send(out_s.at[other], back_s.at[me], RS, other)

        give(b, body)

    loop(blocks, image_block)
    back_b[me] = out_b[me]
    back_s[me] = out_s[me]

    for fetch in fetches[4:]:
        fetch.wait()
    spots = lax.broadcasted_iota(jnp.int32, (rows, 1), 0)

    def start_of(t, column):
        return jnp.where(spots == t, starts[frames[me * rows + t]], column)

    begin = lax.fori_loop(0, rows, start_of, jnp.zeros((rows, 1), jnp.int32))
    audio_rows = audio_kv.shape[0]
    audio_count = n * audio_rows
    slots = lax.broadcasted_iota(jnp.int32, (rows, audio_count), 1)
    inside = (slots >= begin) & (slots < begin + AUD_WIN)
    ranks = audio_q.shape[0]
    inside = jnp.concatenate([inside] * ranks, axis=0)

    drain(gathered.at[pl.ds(0, plane - 1)], recvs.at[NEAR])
    per = 8 // audio_rows

    def widen(g):
        pieces = []
        for i in range(per):
            src = g * per + i
            pieces.append(gathered[src % plane, src // plane].astype(jnp.float32))
        audio_wide[pl.ds(pl.multiple_of(g * 8, 8), 8), :] = jnp.concatenate(pieces, axis=0)

    loop(audio_count // 8, widen)
    def audio_head(h):
        cols = pl.ds(pl.multiple_of(h * dim, dim), dim)
        val_cols = pl.ds(pl.multiple_of(inner + h * dim, dim), dim)
        q = audio_q[:, :, cols].reshape(ranks * rows, dim)
        k = audio_wide[:, cols].astype(jnp.bfloat16)
        v = audio_wide[:, val_cols].astype(jnp.bfloat16)
        s = lax.dot_general(q, k, transposed, preferred_element_type=jnp.float32)
        s = jnp.where(inside, s, -jnp.inf)
        top = jnp.max(s, axis=1, keepdims=True)
        w = jnp.where(inside, jnp.exp2((s - top) * rate), 0.0)
        total = jnp.sum(w, axis=1, keepdims=True)
        o = jnp.dot(w.astype(jnp.bfloat16), v, preferred_element_type=jnp.float32) / total
        audio_out[:, :, cols] = o.reshape(ranks, rows, dim)

    loop(heads, audio_head)

    drain(got_c.at[pl.ds(0, n - 1)], recvs.at[C])

    def plain_block(i):
        b = (turn + i) % blocks
        devices = pl.ds(pl.multiple_of(b * per_block, per_block), per_block)
        q = got_c[devices, :, 0:dim].reshape(q_block, dim)
        k = got_c[:, :, dim : 2 * dim].reshape(n * rows, dim)
        v = got_c[:, :, 2 * dim :].reshape(n * rows, dim)
        o, _, _ = attend(q, (k,), (v,))
        out_c[devices] = o.reshape(per_block, rows, dim)
        give(b, lambda other: send(out_c.at[other], back_c.at[me], RC, other))

    loop(blocks, plain_block)
    back_c[me] = out_c[me]

    swapped = jnp.where(place[0] > place[1], 1, 0)
    seats = (swapped, 1 - swapped)

    def finish(p, result):
        x = hidden[...]
        center = jnp.mean(x, axis=1, keepdims=True)
        x = x - center
        spread = jnp.mean(jnp.square(x), axis=1, keepdims=True)
        x = x * lax.rsqrt(spread + 1e-06)
        gain = modulation[1, pl.ds(place[p], 1), :]
        shift = modulation[0, pl.ds(place[p], 1), :]
        x = (x * (1.0 + gain) + shift).astype(jnp.bfloat16)
        y = lax.dot_general(x, final_weight[...], transposed, preferred_element_type=jnp.float32)
        return result + guide[place[p]].astype(jnp.float32) * y

    result = jnp.zeros(mixed.shape, jnp.float32)
    drain(back_b.at[pl.ds(0, n - 1)], recvs.at[RB])
    drain(back_s.at[pl.ds(0, n - 1)], recvs.at[RS])
    a, b = back_s[0:half, 0, :], back_s[half:n, 0, :]
    most = jnp.maximum(a, b)
    lanes = 4 * rows
    a = jnp.exp2((a - most) * rate) * pltpu.roll(a, lanes - rows, 1)
    b = jnp.exp2((b - most) * rate) * pltpu.roll(b, lanes - rows, 1)
    whole = a + b
    parts = [a / whole, b / whole, jnp.zeros((lanes - n, lanes), jnp.float32)]
    weights[...] = jnp.concatenate(parts, axis=0).T
    for j in range(2):
        p = 2 * j
        tokens = slice(2 * j * rows, (2 * j + 1) * rows)
        for h in range(heads):
            cols = slice(h * dim, (h + 1) * dim)
            x = weights[tokens, h : h + 1] * back_b[h, :, j * dim : (j + 1) * dim].astype(jnp.float32)
            other = half + h
            x = x + weights[tokens, other : other + 1] * back_b[other, :, j * dim : (j + 1) * dim].astype(jnp.float32)
            if PAIRS[p][0]:
                x = x + audio_out[seats[p], :, cols]
            hidden[:, cols] = x
        result = finish(p, result)
    drain(back_c.at[pl.ds(0, n - 1)], recvs.at[RC])
    for j in range(2):
        p = 2 * j + 1
        for h in range(heads):
            cols = slice(h * dim, (h + 1) * dim)
            x = back_c[2 * h + j].astype(jnp.float32)
            if PAIRS[p][0]:
                x = x + audio_out[seats[p], :, cols]
            hidden[:, cols] = x
        result = finish(p, result)
    mixed[...] = result

    drain(gathered.at[0, pl.ds(0, strips - 1)], sends.at[FAR])
    drain(gathered.at[pl.ds(0, plane - 1)], sends.at[NEAR])
    drain(got_q.at[pl.ds(0, n - 1)], sends.at[Q])
    drain(got_k.at[pl.ds(0, half - 1)], sends.at[K])
    drain(got_c.at[pl.ds(0, n - 1)], sends.at[C])
    drain(back_b.at[pl.ds(0, n - 1)], sends.at[RB])
    drain(back_s.at[pl.ds(0, n - 1)], sends.at[RS])
    drain(back_c.at[pl.ds(0, n - 1)], sends.at[RC])


def shards(
    video_heads,
    image_heads,
    audio_queries,
    audio_keys,
    condition_flags,
    guidance_weights,
    token_frame,
    window_start,
    modulation,
    final_weight,
    noisy_latent,
):
    heads, branches, rows, wide = video_heads.shape
    dim = wide // 3
    img_rows = image_heads.shape[2]
    n = lax.axis_size("seq")
    units = heads * branches // n
    assert n & (n - 1) == 0 and units in (1, 2, 4)
    bits = (n - 1).bit_length()
    plane = 2 ** ((bits + 1) // 2)
    tokens = n * rows
    q_block = min(256, tokens)
    images = max(1, units // 2)
    inner = heads * dim
    bf16, f32 = jnp.bfloat16, jnp.float32
    dma = pltpu.SemaphoreType.DMA
    def like(x, space):
        return space(x.shape, x.dtype)

    columns = final_weight.T
    small = (condition_flags, guidance_weights, token_frame, window_start)
    large = (video_heads, image_heads, audio_queries, audio_keys, modulation, columns)
    if 2 * heads == n and branches == 4 and 4 * rows == 128 and rows == 2 * img_rows:
        half = n // 2
        kernel = split_kernel
        working = [
            pltpu.VMEM((heads, rows, 2 * dim), bf16),
            pltpu.VMEM((heads, rows, 6 * dim), bf16),
            pltpu.VMEM((n, rows, wide), bf16),
            pltpu.VMEM((n, rows, 2 * dim), bf16),
            pltpu.VMEM((half, rows, 6 * dim), bf16),
            pltpu.VMEM((n, rows, wide), bf16),
            pltpu.VMEM((n, rows, 2 * dim), bf16),
            pltpu.VMEM((n, 1, 4 * rows), f32),
            pltpu.VMEM((n, rows, dim), bf16),
            pltpu.VMEM((n, rows, 2 * dim), bf16),
            pltpu.VMEM((n, 1, 4 * rows), f32),
            pltpu.VMEM((n, rows, dim), bf16),
            pltpu.VMEM((plane, n // plane) + audio_keys.shape, bf16),
            pltpu.VMEM((n * audio_keys.shape[0], 2 * inner), f32),
            pltpu.VMEM((audio_queries.shape[0], rows, inner), f32),
            pltpu.VMEM((rows, inner), f32),
            pltpu.VMEM((4 * rows, 4 * rows), f32),
            dma((8,)),
            dma((8,)),
        ]
    else:
        kernel = step_kernel
        working = [
            pltpu.VMEM((heads * branches, rows, wide), bf16),
            pltpu.VMEM((heads * branches // 2, img_rows, 2 * dim), bf16),
            pltpu.VMEM((units, tokens, wide), bf16),
            pltpu.VMEM((images, n * img_rows, 2 * dim), bf16),
            pltpu.VMEM((units, tokens, dim), bf16),
            pltpu.VMEM((units, n, rows, dim), bf16),
            pltpu.VMEM((plane, n // plane) + audio_keys.shape, bf16),
            pltpu.VMEM((n * audio_keys.shape[0], 2 * inner), f32),
            pltpu.VMEM((audio_queries.shape[0], rows, inner), f32),
            pltpu.VMEM((rows, inner), f32),
            dma((units,)),
            dma((units,)),
            dma((images,)),
            dma((images,)),
            dma,
            dma,
            dma,
            dma,
            dma((units,)),
            dma((units,)),
        ]
    mixed = pl.pallas_call(
        functools.partial(kernel, n, q_block, plane),
        out_shape=jax.ShapeDtypeStruct(noisy_latent.shape, f32),
        in_specs=[pl.BlockSpec(memory_space=pl.ANY)] * (len(small) + len(large)),
        out_specs=pl.BlockSpec(memory_space=pltpu.VMEM),
        scratch_shapes=[
            *[like(x, pltpu.SMEM) for x in small],
            *[like(x, pltpu.VMEM) for x in large],
            dma((len(small) + len(large),)),
            *working,
        ],
        compiler_params=pltpu.CompilerParams(
            collective_id=0, has_side_effects=True, vmem_limit_bytes=67043328
        ),
        name="avatar_step",
    )(*small, *large)
    velocity = mixed / 8.0
    return (velocity, noisy_latent - 0.125 * velocity)


def solution(mesh):
    in_specs = (
        P("groups", None, "seq", None),
        P("groups", None, "seq", None),
        P("groups", "seq", None),
        P("seq", "groups"),
        P("groups", None),
        P("groups"),
        P("groups"),
        P("groups"),
        P("groups", None, None),
        P(),
        P(("groups", "seq"), None),
    )
    out_specs = (P(("groups", "seq"), None), P(("groups", "seq"), None))
    return jax.shard_map(shards, mesh=mesh, in_specs=in_specs, out_specs=out_specs, check_vma=False)
```

```python
import functools
import math

import jax
import jax.numpy as jnp
from jax import lax
from jax.experimental import pallas as pl
from jax.experimental.pallas import tpu as pltpu
from jax.sharding import PartitionSpec as P

AUD_WIN = 32
PAIRS = ((1, 1), (1, 0), (0, 1), (0, 0))


def step_kernel(
    n,
    q_block,
    plane,
    flags_in,
    guide_in,
    frames_in,
    starts_in,
    video_in,
    image_in,
    audio_q_in,
    audio_kv_in,
    modulation_in,
    final_weight_in,
    mixed,
    flags,
    guide,
    frames,
    starts,
    video,
    image,
    audio_q,
    audio_kv,
    modulation,
    final_weight,
    loads,
    staged,
    staged_img,
    got,
    got_img,
    outs,
    back,
    gathered,
    audio_wide,
    audio_out,
    hidden,
    send_v,
    recv_v,
    send_i,
    recv_i,
    send_a,
    recv_a,
    send_b,
    recv_b,
    send_o,
    recv_o,
):
    heads, branches, rows, wide = video.shape
    dim = wide // 3
    img_rows = image.shape[2]
    inner = heads * dim
    units = heads * branches // n
    tokens = n * rows
    me = lax.axis_index("seq")
    bits = (n - 1).bit_length()
    flips = [(1 - 2 * ((me // 2**i) % 2)) * 2**i for i in range(bits)]

    def partner(k):
        other = me
        for i in range(bits):
            other = other + ((k // 2**i) % 2) * flips[i]
        return other

    def each_peer(body):
        def step(i, carry):
            body(partner(n - 1 - i))
            return carry

        lax.fori_loop(0, n - 1, step, 0)

    def send(src, dst, s_sem, r_sem, other):
        pltpu.make_async_remote_copy(
            src_ref=src,
            dst_ref=dst,
            send_sem=s_sem,
            recv_sem=r_sem,
            device_id={"seq": other},
            device_id_type=pl.DeviceIdType.MESH,
        ).start()

    def drain(ref, sem):
        pltpu.make_async_copy(ref, ref, sem).wait()

    pairs = (
        (flags_in, flags),
        (video_in, video),
        (image_in, image),
        (audio_kv_in, audio_kv),
        (frames_in, frames),
        (starts_in, starts),
        (guide_in, guide),
        (audio_q_in, audio_q),
        (modulation_in, modulation),
        (final_weight_in, final_weight),
    )
    fetches = [pltpu.make_async_copy(src, dst, loads.at[i]) for i, (src, dst) in enumerate(pairs)]
    for fetch in fetches:
        fetch.start()

    barrier = pltpu.get_barrier_semaphore()
    each_peer(
        lambda other: pl.semaphore_signal(
            barrier, inc=1, device_id={"seq": other}, device_id_type=pl.DeviceIdType.MESH
        )
    )

    for fetch in fetches[:4]:
        fetch.wait()
    place = []
    for aud, img in PAIRS:
        at = jnp.int32(0)
        for b in range(branches):
            f0, f1 = flags[0, b], flags[1, b]
            at = at + b * ((f0 if aud else 1 - f0) * (f1 if img else 1 - f1))
        place.append(jnp.minimum(at, branches - 1))

    def stage(h, carry):
        for p in range(branches):
            staged[h * branches + p] = video[h, place[p]]
        for p in range(0, branches, 2):
            staged_img[h * (branches // 2) + p // 2] = image[h, place[p]]
        return carry

    lax.fori_loop(0, heads, stage, 0)
    pl.semaphore_wait(barrier, n - 1)

    mine = pl.ds(pl.multiple_of(me * rows, rows), rows)
    mine_img = pl.ds(pl.multiple_of(me * img_rows, img_rows), img_rows)

    strips = n // plane
    my_strip, my_seat = me // plane, me % plane
    pltpu.sync_copy(audio_kv, gathered.at[my_seat, my_strip])

    def far(i, carry):
        strip = (my_strip + 1 + i) % strips
        send(
            audio_kv,
            gathered.at[my_seat, my_strip],
            send_a,
            recv_a,
            strip * plane + my_seat,
        )
        return carry

    lax.fori_loop(0, strips - 1, far, 0)

    def send_unit(j):
        each_peer(
            lambda other: send(
                staged.at[other * units + j], got.at[j, mine], send_v.at[j], recv_v.at[j], other
            )
        )

    def send_image(m):
        def one(other):
            if units > 1:
                item = other * (units // 2) + m
                send(staged_img.at[item], got_img.at[m, mine_img], send_i.at[m], recv_i.at[m], other)
            else:

                @pl.when(other % 2 == 0)
                def _():
                    send(
                        staged_img.at[other // 2],
                        got_img.at[m, mine_img],
                        send_i.at[m],
                        recv_i.at[m],
                        other,
                    )

        each_peer(one)

    send_unit(0)
    send_image(0)
    drain(gathered.at[0, pl.ds(0, strips - 1)], recv_a)

    def near(i, carry):
        seat = (my_seat + 1 + i) % plane
        send(
            gathered.at[my_seat], gathered.at[my_seat], send_b, recv_b, my_strip * plane + seat
        )
        return carry

    lax.fori_loop(0, plane - 1, near, 0)
    for j in range(1, units):
        send_unit(j)
        if j % 2 == 0:
            send_image(j // 2)

    for j in range(units):
        got[j, mine] = staged[me * units + j]
    if units > 1:
        for m in range(units // 2):
            got_img[m, mine_img] = staged_img[me * (units // 2) + m]
    else:

        @pl.when(me % 2 == 0)
        def _():
            got_img[0, mine_img] = staged_img[me // 2]

    for fetch in fetches[4:]:
        fetch.wait()
    spots = lax.broadcasted_iota(jnp.int32, (rows, 1), 0)

    def start_of(t, column):
        return jnp.where(spots == t, starts[frames[me * rows + t]], column)

    first = lax.fori_loop(0, rows, start_of, jnp.zeros((rows, 1), jnp.int32))
    audio_rows = audio_kv.shape[0]
    audio_count = n * audio_rows
    slots = lax.broadcasted_iota(jnp.int32, (rows, audio_count), 1)
    inside = (slots >= first) & (slots < first + AUD_WIN)
    ranks = audio_q.shape[0]
    inside = jnp.concatenate([inside] * ranks, axis=0)

    drain(gathered.at[pl.ds(0, plane - 1)], recv_b)
    per = 8 // audio_rows

    def widen(g, carry):
        pieces = []
        for i in range(per):
            src = g * per + i
            pieces.append(gathered[src % plane, src // plane].astype(jnp.float32))
        audio_wide[pl.ds(pl.multiple_of(g * 8, 8), 8), :] = jnp.concatenate(pieces, axis=0)
        return carry

    lax.fori_loop(0, audio_count // 8, widen, 0)
    scale = 1.0 / math.sqrt(dim)
    log2e = math.log2(math.e)
    transposed = (((1,), (1,)), ((), ()))

    def audio_head(h, carry):
        cols = pl.ds(pl.multiple_of(h * dim, dim), dim)
        val_cols = pl.ds(pl.multiple_of(inner + h * dim, dim), dim)
        q = audio_q[:, :, cols].reshape(ranks * rows, dim)
        k = audio_wide[:, cols].astype(jnp.bfloat16)
        v = audio_wide[:, val_cols].astype(jnp.bfloat16)
        s = lax.dot_general(q, k, transposed, preferred_element_type=jnp.float32)
        s = jnp.where(inside, s, -jnp.inf)
        top = jnp.max(s, axis=1, keepdims=True)
        w = jnp.where(inside, jnp.exp2((s - top) * (scale * log2e)), 0.0)
        total = jnp.sum(w, axis=1, keepdims=True)
        o = jnp.dot(w.astype(jnp.bfloat16), v, preferred_element_type=jnp.float32) / total
        audio_out[:, :, cols] = o.reshape(ranks, rows, dim)
        return carry

    lax.fori_loop(0, heads, audio_head, 0)

    blocks = tokens // q_block
    per_block = q_block // rows
    turn = me // per_block + 1

    def attend(j, with_image):
        def block(i, carry):
            b = (turn + i) % blocks
            at = pl.ds(pl.multiple_of(b * q_block, q_block), q_block)
            q = got[j, at, 0:dim]
            k = got[j, :, dim : 2 * dim]
            v = got[j, :, 2 * dim :]
            s = lax.dot_general(q, k, transposed, preferred_element_type=jnp.float32)
            top = jnp.max(s, axis=1, keepdims=True)
            if with_image:
                ki = got_img[j // 2, :, 0:dim]
                vi = got_img[j // 2, :, dim:]
                si = lax.dot_general(q, ki, transposed, preferred_element_type=jnp.float32)
                top = jnp.maximum(top, jnp.max(si, axis=1, keepdims=True))
            w = jnp.exp2((s - top) * (scale * log2e))
            total = jnp.sum(w, axis=1, keepdims=True)
            o = jnp.dot(w.astype(jnp.bfloat16), v, preferred_element_type=jnp.float32)
            if with_image:
                wi = jnp.exp2((si - top) * (scale * log2e))
                total = total + jnp.sum(wi, axis=1, keepdims=True)
                o = o + jnp.dot(wi.astype(jnp.bfloat16), vi, preferred_element_type=jnp.float32)
            outs[j, at, :] = (o / total).astype(jnp.bfloat16)

            def give(d, inner_carry):
                other = b * per_block + d
                part = outs.at[j, pl.ds(pl.multiple_of(other * rows, rows), rows)]

                @pl.when(other != me)
                def _():
                    send(part, back.at[j, me], send_o.at[j], recv_o.at[j], other)

                return inner_carry

            lax.fori_loop(0, per_block, give, 0)
            return carry

        lax.fori_loop(0, blocks, block, 0)
        back[j, me] = outs[j, mine, :]

    for j in range(units):
        drain(got.at[j, pl.ds(0, (n - 1) * rows)], recv_v.at[j])
        if units > 1:
            if j % 2 == 0:
                drain(got_img.at[j // 2, pl.ds(0, (n - 1) * img_rows)], recv_i.at[j // 2])
            attend(j, j % 2 == 0)
        else:

            @pl.when(me % 2 == 0)
            def _():
                drain(got_img.at[0, pl.ds(0, (n - 1) * img_rows)], recv_i.at[0])
                attend(0, True)

            @pl.when(me % 2 == 1)
            def _():
                attend(0, False)

    swapped = jnp.where(place[0] > place[1], 1, 0)
    seats = (swapped, 1 - swapped)
    result = jnp.zeros(mixed.shape, jnp.float32)
    for j in range(units):
        drain(back.at[j, pl.ds(0, n - 1)], recv_o.at[j])
        for p in range(j, branches, units):
            for h in range(heads):
                cols = slice(h * dim, (h + 1) * dim)
                x = back[j, (h * branches + p) // units].astype(jnp.float32)
                if PAIRS[p][0]:
                    x = x + audio_out[seats[p], :, cols]
                hidden[:, cols] = x
            x = hidden[...]
            center = jnp.mean(x, axis=1, keepdims=True)
            x = x - center
            spread = jnp.mean(jnp.square(x), axis=1, keepdims=True)
            x = x * lax.rsqrt(spread + 1e-06)
            gain = modulation[1, pl.ds(place[p], 1), :]
            shift = modulation[0, pl.ds(place[p], 1), :]
            x = (x * (1.0 + gain) + shift).astype(jnp.bfloat16)
            y = lax.dot_general(x, final_weight[...], transposed, preferred_element_type=jnp.float32)
            result = result + guide[place[p]].astype(jnp.float32) * y
    mixed[...] = result

    drain(gathered.at[0, pl.ds(0, strips - 1)], send_a)
    drain(gathered.at[pl.ds(0, plane - 1)], send_b)
    for j in range(units):
        drain(staged.at[pl.ds(0, n - 1)], send_v.at[j])
        drain(back.at[j, pl.ds(0, n - 1)], send_o.at[j])
    if units > 1:
        for m in range(units // 2):
            drain(staged_img.at[pl.ds(0, n - 1)], send_i.at[m])
    else:

        @pl.when(me % 2 == 0)
        def _():
            drain(staged_img.at[pl.ds(0, n // 2 - 1)], send_i.at[0])

        @pl.when(me % 2 == 1)
        def _():
            drain(staged_img.at[pl.ds(0, n // 2)], send_i.at[0])


def split_kernel(
    n,
    q_block,
    plane,
    flags_in,
    guide_in,
    frames_in,
    starts_in,
    video_in,
    image_in,
    audio_q_in,
    audio_kv_in,
    modulation_in,
    final_weight_in,
    mixed,
    flags,
    guide,
    frames,
    starts,
    video,
    image,
    audio_q,
    audio_kv,
    modulation,
    final_weight,
    loads,
    st_q,
    st_k,
    st_c,
    got_q,
    got_k,
    got_c,
    out_b,
    out_s,
    out_c,
    out_y,
    out_z,
    back_b,
    back_s,
    back_c,
    back_y,
    back_z,
    gathered,
    audio_wide,
    audio_out,
    hidden,
    weights,
    folded,
    sends,
    recvs,
    ready,
):
    heads, branches, rows, wide = video.shape
    dim = wide // 3
    img_rows = image.shape[2]
    inner = heads * dim
    half = n // 2
    quarter = n // 4
    channels = final_weight.shape[0]
    me = lax.axis_index("seq")
    loc = me % half
    bits = (n - 1).bit_length()
    flips = [(1 - 2 * ((me // 2**i) % 2)) * 2**i for i in range(bits)]

    def partner(k):
        other = me
        for i in range(bits):
            other = other + ((k // 2**i) % 2) * flips[i]
        return other

    def loop(count, body):
        def step(i, carry):
            body(i)
            return carry

        lax.fori_loop(0, count, step, 0)

    def send(src, dst, which, other):
        pltpu.make_async_remote_copy(
            src_ref=src,
            dst_ref=dst,
            send_sem=sends.at[which],
            recv_sem=recvs.at[which],
            device_id={"seq": other},
            device_id_type=pl.DeviceIdType.MESH,
        ).start()

    def drain(ref, sem):
        pltpu.make_async_copy(ref, ref, sem).wait()

    Q, K, C, FAR, NEAR, RB, RS, RC, RY, RZ = range(10)

    central = (me >= quarter) & (me < half + quarter)
    my_head = jnp.where(central, me - quarter, jnp.where(me < quarter, me, me - half))

    kin = [k for k in range(n - 1, 0, -1) if k < plane or k % plane < 2]
    rest = [k for k in range(n - 1, 0, -1) if k not in kin]

    def greet(sem):
        for k in kin:
            pl.semaphore_signal(
                sem, inc=1, device_id={"seq": partner(k)}, device_id_type=pl.DeviceIdType.MESH
            )

    barrier = pltpu.get_barrier_semaphore()
    greet(barrier)
    pairs = (
        (flags_in, flags),
        (video_in, video),
        (image_in, image),
        (audio_kv_in, audio_kv),
        (frames_in, frames),
        (starts_in, starts),
        (guide_in, guide),
        (audio_q_in, audio_q),
        (modulation_in, modulation),
        (final_weight_in, final_weight),
    )
    fetches = [pltpu.make_async_copy(src, dst, loads.at[i]) for i, (src, dst) in enumerate(pairs)]
    for fetch in fetches:
        fetch.start()
    for fetch in fetches[:4]:
        fetch.wait()
    place = []
    for aud, img in PAIRS:
        at = jnp.int32(0)
        for b in range(branches):
            f0, f1 = flags[0, b], flags[1, b]
            at = at + b * ((f0 if aud else 1 - f0) * (f1 if img else 1 - f1))
        place.append(jnp.minimum(at, branches - 1))

    def stage(h):
        for j in range(2):
            x = video[h, place[2 * j]]
            st_q[h, :, j * dim : (j + 1) * dim] = x[:, :dim]
            st_k[h, :, 2 * j * dim : 2 * (j + 1) * dim] = x[:, dim:]
            st_k[h, j * img_rows : (j + 1) * img_rows, 4 * dim :] = image[h, place[2 * j]]
        st_c[quarter + h] = video[h, place[1]]
        st_c[h + jnp.where(h < quarter, 0, half)] = video[h, place[3]]

    loop(heads, stage)
    pl.semaphore_wait(barrier, len(kin))
    greet(ready)

    strips = n // plane
    my_strip, my_seat = me // plane, me % plane
    pltpu.sync_copy(audio_kv, gathered.at[my_seat, my_strip])

    def far(i):
        strip = (my_strip + 1 + i) % strips
        send(audio_kv, gathered.at[my_seat, my_strip], FAR, strip * plane + my_seat)

    loop(strips - 1, far)

    def send_q(other):
        send(st_q.at[other % half], got_q.at[me], Q, other)

    def send_k(other):
        send(st_k.at[other % half], got_k.at[loc], K, other)

    def send_c(other):
        send(st_c.at[other], got_c.at[me], C, other)

    def mixed_order(ks):
        cross, same = [k for k in ks if k >= half], [k for k in ks if k < half]
        for i in range(max(len(cross), len(same))):
            yield from cross[i : i + 1] + same[i : i + 1]

    def first(ks):
        for k in mixed_order(ks):
            other = partner(k)
            if k < half:
                send_k(other)
            send_q(other)

    first(kin)
    pl.semaphore_wait(ready, len(kin))
    first(rest)
    drain(gathered.at[0, pl.ds(0, strips - 1)], recvs.at[FAR])

    def near(i):
        seat = (my_seat + 1 + i) % plane
        send(gathered.at[my_seat], gathered.at[my_seat], NEAR, my_strip * plane + seat)

    loop(plane - 1, near)

    def second(i):
        send_c(partner(n - 1 - i))

    loop(n - 1, second)

    got_q[me] = st_q[loc]
    got_k[loc] = st_k[loc]
    got_c[me] = st_c[me]

    scale = 1.0 / math.sqrt(dim)
    rate = scale * math.log2(math.e)
    transposed = (((1,), (1,)), ((), ()))

    blocks = n * rows // q_block
    per_block = q_block // rows
    turn = me // per_block + 1

    def attend(q, keys, values):
        scores = [lax.dot_general(q, k, transposed, preferred_element_type=jnp.float32) for k in keys]
        top = functools.reduce(jnp.maximum, [jnp.max(s, axis=1, keepdims=True) for s in scores])
        total, o = 0.0, 0.0
        for s, v in zip(scores, values):
            w = jnp.exp2((s - top) * rate)
            total = total + jnp.sum(w, axis=1, keepdims=True)
            o = o + jnp.dot(w.astype(jnp.bfloat16), v, preferred_element_type=jnp.float32)
        return (o / total).astype(jnp.bfloat16), top, total

    def give(b, body):
        def one(d):
            other = b * per_block + d

            @pl.when(other != me)
            def _():
                body(other)

        loop(per_block, one)

    for fetch in fetches[4:]:
        fetch.wait()
    drain(got_q.at[pl.ds(0, n - 1)], recvs.at[Q])
    drain(got_k.at[pl.ds(0, half - 1)], recvs.at[K])

    lane = lax.broadcasted_iota(jnp.int32, (q_block, 4 * rows), 1)
    diagonal = lane % rows == lax.broadcasted_iota(jnp.int32, (q_block, 4 * rows), 0) % rows

    head_of = lax.broadcasted_iota(jnp.int32, (folded.shape[0], inner), 1) // dim
    line = lax.broadcasted_iota(jnp.int32, (folded.shape[0], inner), 0)
    gains = 1.0 + modulation[1, pl.ds(place[3], 1), :]
    table = jnp.where(line == head_of, gains, jnp.where(line == heads, modulation[0, pl.ds(place[3], 1), :], 0.0))
    folded[...] = lax.dot_general(
        table,
        final_weight[...].astype(jnp.float32),
        transposed,
        precision=lax.Precision.HIGHEST,
        preferred_element_type=jnp.float32,
    )

    def image_block(i):
        b = (turn + i) % blocks
        devices = pl.ds(pl.multiple_of(b * per_block, per_block), per_block)
        stats = []
        for j in range(2):
            q = got_q[devices, :, j * dim : (j + 1) * dim].reshape(q_block, dim)
            at = 2 * j * dim
            k = got_k[:, :, at : at + dim].reshape(half * rows, dim)
            v = got_k[:, :, at + dim : at + 2 * dim].reshape(half * rows, dim)
            pick = slice(j * img_rows, (j + 1) * img_rows)
            ki = got_k[:, pick, 4 * dim : 5 * dim].reshape(half * img_rows, dim)
            vi = got_k[:, pick, 5 * dim :].reshape(half * img_rows, dim)
            o, top, total = attend(q, (k, ki), (v, vi))
            out_b[devices, :, j * dim : (j + 1) * dim] = o.reshape(per_block, rows, dim)
            stats += [top, total]
        x = jnp.where(lane < rows, stats[0], jnp.where(lane < 2 * rows, stats[1], jnp.where(lane < 3 * rows, stats[2], stats[3])))
        x = jnp.where(diagonal, x, 0.0).reshape(per_block, rows, 4 * rows)
        out_s[devices, 0, :] = jnp.sum(x, axis=1)

        def body(other):
            send(out_b.at[other], back_b.at[me], RB, other)
            send(out_s.at[other], back_s.at[me], RS, other)

        give(b, body)

    loop(blocks, image_block)
    back_b[me] = out_b[me]
    back_s[me] = out_s[me]

    spots = lax.broadcasted_iota(jnp.int32, (rows, 1), 0)

    def start_of(t, column):
        return jnp.where(spots == t, starts[frames[me * rows + t]], column)

    begin = lax.fori_loop(0, rows, start_of, jnp.zeros((rows, 1), jnp.int32))
    audio_rows = audio_kv.shape[0]
    audio_count = n * audio_rows
    slots = lax.broadcasted_iota(jnp.int32, (rows, audio_count), 1)
    inside = (slots >= begin) & (slots < begin + AUD_WIN)
    ranks = audio_q.shape[0]
    inside = jnp.concatenate([inside] * ranks, axis=0)

    drain(gathered.at[pl.ds(0, plane - 1)], recvs.at[NEAR])
    per = 8 // audio_rows

    def widen(g):
        pieces = []
        for i in range(per):
            src = g * per + i
            pieces.append(gathered[src % plane, src // plane].astype(jnp.float32))
        audio_wide[pl.ds(pl.multiple_of(g * 8, 8), 8), :] = jnp.concatenate(pieces, axis=0)

    loop(audio_count // 8, widen)
    def audio_head(h):
        cols = pl.ds(pl.multiple_of(h * dim, dim), dim)
        val_cols = pl.ds(pl.multiple_of(inner + h * dim, dim), dim)
        q = audio_q[:, :, cols].reshape(ranks * rows, dim)
        k = audio_wide[:, cols].astype(jnp.bfloat16)
        v = audio_wide[:, val_cols].astype(jnp.bfloat16)
        s = lax.dot_general(q, k, transposed, preferred_element_type=jnp.float32)
        s = jnp.where(inside, s, -jnp.inf)
        top = jnp.max(s, axis=1, keepdims=True)
        w = jnp.where(inside, jnp.exp2((s - top) * rate), 0.0)
        total = jnp.sum(w, axis=1, keepdims=True)
        o = jnp.dot(w.astype(jnp.bfloat16), v, preferred_element_type=jnp.float32) / total
        audio_out[:, :, cols] = o.reshape(ranks, rows, dim)

    loop(heads // 2, audio_head)

    drain(got_c.at[pl.ds(0, n - 1)], recvs.at[C])

    def plain_block(i):
        b = (turn + i) % blocks
        devices = pl.ds(pl.multiple_of(b * per_block, per_block), per_block)
        q = got_c[devices, :, 0:dim].reshape(q_block, dim)
        k = got_c[:, :, dim : 2 * dim].reshape(n * rows, dim)
        v = got_c[:, :, 2 * dim :].reshape(n * rows, dim)
        o, _, _ = attend(q, (k,), (v,))

        @pl.when(central)
        def _():
            out_c[devices] = o.reshape(per_block, rows, dim)
            give(b, lambda other: send(out_c.at[other], back_c.at[my_head], RC, other))

        @pl.when(jnp.logical_not(central))
        def _():
            x = o.astype(jnp.float32)
            center = jnp.mean(x, axis=1, keepdims=True)
            x = x - center
            spread = jnp.sum(jnp.square(x), axis=1, keepdims=True)
            cols = pl.ds(pl.multiple_of(my_head * dim, dim), dim)
            chosen = lax.broadcasted_iota(jnp.int32, (branches, dim), 0) == place[3]
            gain = jnp.sum(jnp.where(chosen, modulation[1, :, cols], 0.0), axis=0, keepdims=True)
            x = (x * (1.0 + gain)).astype(jnp.bfloat16)
            y = lax.dot_general(x, final_weight[:, cols], transposed, preferred_element_type=jnp.float32)
            y = y.reshape(per_block, rows, channels)
            y = jnp.concatenate([y[:, : rows // 2], y[:, rows // 2 :]], axis=2)
            out_y[devices] = y.astype(jnp.bfloat16)
            z = jnp.where(lane < rows, center, jnp.where(lane < 2 * rows, spread, 0.0))
            z = jnp.where(diagonal, z, 0.0).reshape(per_block, rows, 4 * rows)
            out_z[devices, 0, :] = jnp.sum(z, axis=1)

            def body(other):
                send(out_y.at[other], back_y.at[my_head], RY, other)
                send(out_z.at[other], back_z.at[my_head], RZ, other)

            give(b, body)

    loop(blocks, plain_block)

    @pl.when(central)
    def _():
        back_c[my_head] = out_c[me]

    @pl.when(jnp.logical_not(central))
    def _():
        back_y[my_head] = out_y[me]
        back_z[my_head] = out_z[me]

    loop(heads - heads // 2, lambda i: audio_head(heads // 2 + i))
    swapped = jnp.where(place[0] > place[1], 1, 0)
    seats = (swapped, 1 - swapped)

    def finish(p, result):
        x = hidden[...]
        center = jnp.mean(x, axis=1, keepdims=True)
        x = x - center
        spread = jnp.mean(jnp.square(x), axis=1, keepdims=True)
        x = x * lax.rsqrt(spread + 1e-06)
        gain = modulation[1, pl.ds(place[p], 1), :]
        shift = modulation[0, pl.ds(place[p], 1), :]
        x = (x * (1.0 + gain) + shift).astype(jnp.bfloat16)
        y = lax.dot_general(x, final_weight[...], transposed, preferred_element_type=jnp.float32)
        return result + guide[place[p]].astype(jnp.float32) * y

    result = jnp.zeros(mixed.shape, jnp.float32)
    drain(back_b.at[pl.ds(0, n - 1)], recvs.at[RB])
    drain(back_s.at[pl.ds(0, n - 1)], recvs.at[RS])
    a, b = back_s[0:half, 0, :], back_s[half:n, 0, :]
    most = jnp.maximum(a, b)
    lanes = 4 * rows
    a = jnp.exp2((a - most) * rate) * pltpu.roll(a, lanes - rows, 1)
    b = jnp.exp2((b - most) * rate) * pltpu.roll(b, lanes - rows, 1)
    whole = a + b
    parts = [a / whole, b / whole, jnp.zeros((lanes - n, lanes), jnp.float32)]
    weights[...] = jnp.concatenate(parts, axis=0).T
    for j in range(2):
        p = 2 * j
        tokens = slice(2 * j * rows, (2 * j + 1) * rows)
        for h in range(heads):
            cols = slice(h * dim, (h + 1) * dim)
            x = weights[tokens, h : h + 1] * back_b[h, :, j * dim : (j + 1) * dim].astype(jnp.float32)
            other = half + h
            x = x + weights[tokens, other : other + 1] * back_b[other, :, j * dim : (j + 1) * dim].astype(jnp.float32)
            if PAIRS[p][0]:
                x = x + audio_out[seats[p], :, cols]
            hidden[:, cols] = x
        result = finish(p, result)

    @pl.when(central)
    def _():
        drain(back_c.at[pl.ds(0, heads - 1)], recvs.at[RC])
        drain(back_y, recvs.at[RY])
        drain(back_z, recvs.at[RZ])

    @pl.when(jnp.logical_not(central))
    def _():
        drain(back_c, recvs.at[RC])
        drain(back_y.at[pl.ds(0, heads - 1)], recvs.at[RY])
        drain(back_z.at[pl.ds(0, heads - 1)], recvs.at[RZ])

    for h in range(heads):
        cols = slice(h * dim, (h + 1) * dim)
        hidden[:, cols] = back_c[h].astype(jnp.float32) + audio_out[seats[1], :, cols]
    result = finish(1, result)
    z = back_z[:, 0, :]
    center = jnp.mean(z, axis=0, keepdims=True)
    away = z - center
    spread = jnp.sum(pltpu.roll(z, lanes - rows, 1) + dim * jnp.square(away), axis=0, keepdims=True) / inner
    parts = [away, lax.rsqrt(spread + 1e-06), jnp.zeros((lanes - heads - 1, lanes), jnp.float32)]
    weights[...] = jnp.concatenate(parts, axis=0).T
    y = functools.reduce(jnp.add, [back_y[h].astype(jnp.float32) for h in range(heads)])
    y = jnp.concatenate([y[:, :channels], y[:, channels:]], axis=0)
    for h in range(heads):
        y = y + weights[0:rows, h : h + 1] * folded[h : h + 1, :]
    y = weights[0:rows, heads : heads + 1] * y + folded[heads : heads + 1, :]
    result = result + guide[place[3]].astype(jnp.float32) * y
    mixed[...] = result

    drain(gathered.at[0, pl.ds(0, strips - 1)], sends.at[FAR])
    drain(gathered.at[pl.ds(0, plane - 1)], sends.at[NEAR])
    drain(got_q.at[pl.ds(0, n - 1)], sends.at[Q])
    drain(got_k.at[pl.ds(0, half - 1)], sends.at[K])
    drain(got_c.at[pl.ds(0, n - 1)], sends.at[C])
    drain(back_b.at[pl.ds(0, n - 1)], sends.at[RB])
    drain(back_s.at[pl.ds(0, n - 1)], sends.at[RS])

    @pl.when(central)
    def _():
        drain(out_c.at[pl.ds(0, n - 1)], sends.at[RC])

    @pl.when(jnp.logical_not(central))
    def _():
        drain(out_y.at[pl.ds(0, n - 1)], sends.at[RY])
        drain(out_z.at[pl.ds(0, n - 1)], sends.at[RZ])


def shards(
    video_heads,
    image_heads,
    audio_queries,
    audio_keys,
    condition_flags,
    guidance_weights,
    token_frame,
    window_start,
    modulation,
    final_weight,
    noisy_latent,
):
    heads, branches, rows, wide = video_heads.shape
    dim = wide // 3
    img_rows = image_heads.shape[2]
    n = lax.axis_size("seq")
    units = heads * branches // n
    assert n & (n - 1) == 0 and units in (1, 2, 4)
    bits = (n - 1).bit_length()
    plane = 2 ** ((bits + 1) // 2)
    tokens = n * rows
    q_block = min(256, tokens)
    images = max(1, units // 2)
    inner = heads * dim
    bf16, f32 = jnp.bfloat16, jnp.float32
    dma = pltpu.SemaphoreType.DMA
    def like(x, space):
        return space(x.shape, x.dtype)

    columns = final_weight.T
    small = (condition_flags, guidance_weights, token_frame, window_start)
    large = (video_heads, image_heads, audio_queries, audio_keys, modulation, columns)
    channels = final_weight.shape[1]
    if 2 * heads == n and branches == 4 and 4 * rows == 128 and rows == 2 * img_rows and channels == 64:
        half = n // 2
        kernel = split_kernel
        working = [
            pltpu.VMEM((heads, rows, 2 * dim), bf16),
            pltpu.VMEM((heads, rows, 6 * dim), bf16),
            pltpu.VMEM((n, rows, wide), bf16),
            pltpu.VMEM((n, rows, 2 * dim), bf16),
            pltpu.VMEM((half, rows, 6 * dim), bf16),
            pltpu.VMEM((n, rows, wide), bf16),
            pltpu.VMEM((n, rows, 2 * dim), bf16),
            pltpu.VMEM((n, 1, 4 * rows), f32),
            pltpu.VMEM((n, rows, dim), bf16),
            pltpu.VMEM((n, rows // 2, 2 * channels), bf16),
            pltpu.VMEM((n, 1, 4 * rows), f32),
            pltpu.VMEM((n, rows, 2 * dim), bf16),
            pltpu.VMEM((n, 1, 4 * rows), f32),
            pltpu.VMEM((heads, rows, dim), bf16),
            pltpu.VMEM((heads, rows // 2, 2 * channels), bf16),
            pltpu.VMEM((heads, 1, 4 * rows), f32),
            pltpu.VMEM((plane, n // plane) + audio_keys.shape, bf16),
            pltpu.VMEM((n * audio_keys.shape[0], 2 * inner), f32),
            pltpu.VMEM((audio_queries.shape[0], rows, inner), f32),
            pltpu.VMEM((rows, inner), f32),
            pltpu.VMEM((4 * rows, 4 * rows), f32),
            pltpu.VMEM((-(-(heads + 1) // 8) * 8, channels), f32),
            dma((10,)),
            dma((10,)),
            pltpu.SemaphoreType.REGULAR,
        ]
    else:
        kernel = step_kernel
        working = [
            pltpu.VMEM((heads * branches, rows, wide), bf16),
            pltpu.VMEM((heads * branches // 2, img_rows, 2 * dim), bf16),
            pltpu.VMEM((units, tokens, wide), bf16),
            pltpu.VMEM((images, n * img_rows, 2 * dim), bf16),
            pltpu.VMEM((units, tokens, dim), bf16),
            pltpu.VMEM((units, n, rows, dim), bf16),
            pltpu.VMEM((plane, n // plane) + audio_keys.shape, bf16),
            pltpu.VMEM((n * audio_keys.shape[0], 2 * inner), f32),
            pltpu.VMEM((audio_queries.shape[0], rows, inner), f32),
            pltpu.VMEM((rows, inner), f32),
            dma((units,)),
            dma((units,)),
            dma((images,)),
            dma((images,)),
            dma,
            dma,
            dma,
            dma,
            dma((units,)),
            dma((units,)),
        ]
    mixed = pl.pallas_call(
        functools.partial(kernel, n, q_block, plane),
        out_shape=jax.ShapeDtypeStruct(noisy_latent.shape, f32),
        in_specs=[pl.BlockSpec(memory_space=pl.ANY)] * (len(small) + len(large)),
        out_specs=pl.BlockSpec(memory_space=pltpu.VMEM),
        scratch_shapes=[
            *[like(x, pltpu.SMEM) for x in small],
            *[like(x, pltpu.VMEM) for x in large],
            dma((len(small) + len(large),)),
            *working,
        ],
        compiler_params=pltpu.CompilerParams(
            collective_id=0, has_side_effects=True, vmem_limit_bytes=67043328
        ),
        name="avatar_step",
    )(*small, *large)
    velocity = mixed / 8.0
    return (velocity, noisy_latent - 0.125 * velocity)


def solution(mesh):
    in_specs = (
        P("groups", None, "seq", None),
        P("groups", None, "seq", None),
        P("groups", "seq", None),
        P("seq", "groups"),
        P("groups", None),
        P("groups"),
        P("groups"),
        P("groups"),
        P("groups", None, None),
        P(),
        P(("groups", "seq"), None),
    )
    out_specs = (P(("groups", "seq"), None), P(("groups", "seq"), None))
    return jax.shard_map(shards, mesh=mesh, in_specs=in_specs, out_specs=out_specs, check_vma=False)
```

```python
import functools
import math

import jax
import jax.numpy as jnp
from jax import lax
from jax.experimental import pallas as pl
from jax.experimental.pallas import tpu as pltpu
from jax.sharding import PartitionSpec as P

AUD_WIN = 32
PAIRS = ((1, 1), (1, 0), (0, 1), (0, 0))


def step_kernel(
    n,
    q_block,
    plane,
    flags_in,
    guide_in,
    frames_in,
    starts_in,
    video_in,
    image_in,
    audio_q_in,
    audio_kv_in,
    modulation_in,
    final_weight_in,
    mixed,
    flags,
    guide,
    frames,
    starts,
    video,
    image,
    audio_q,
    audio_kv,
    modulation,
    final_weight,
    loads,
    staged,
    staged_img,
    got,
    got_img,
    outs,
    back,
    gathered,
    audio_wide,
    audio_out,
    hidden,
    send_v,
    recv_v,
    send_i,
    recv_i,
    send_a,
    recv_a,
    send_b,
    recv_b,
    send_o,
    recv_o,
):
    heads, branches, rows, wide = video.shape
    dim = wide // 3
    img_rows = image.shape[2]
    inner = heads * dim
    units = heads * branches // n
    tokens = n * rows
    me = lax.axis_index("seq")
    bits = (n - 1).bit_length()
    flips = [(1 - 2 * ((me // 2**i) % 2)) * 2**i for i in range(bits)]

    def partner(k):
        other = me
        for i in range(bits):
            other = other + ((k // 2**i) % 2) * flips[i]
        return other

    def each_peer(body):
        def step(i, carry):
            body(partner(n - 1 - i))
            return carry

        lax.fori_loop(0, n - 1, step, 0)

    def send(src, dst, s_sem, r_sem, other):
        pltpu.make_async_remote_copy(
            src_ref=src,
            dst_ref=dst,
            send_sem=s_sem,
            recv_sem=r_sem,
            device_id={"seq": other},
            device_id_type=pl.DeviceIdType.MESH,
        ).start()

    def drain(ref, sem):
        pltpu.make_async_copy(ref, ref, sem).wait()

    pairs = (
        (flags_in, flags),
        (video_in, video),
        (image_in, image),
        (audio_kv_in, audio_kv),
        (frames_in, frames),
        (starts_in, starts),
        (guide_in, guide),
        (audio_q_in, audio_q),
        (modulation_in, modulation),
        (final_weight_in, final_weight),
    )
    fetches = [pltpu.make_async_copy(src, dst, loads.at[i]) for i, (src, dst) in enumerate(pairs)]
    for fetch in fetches:
        fetch.start()

    barrier = pltpu.get_barrier_semaphore()
    each_peer(
        lambda other: pl.semaphore_signal(
            barrier, inc=1, device_id={"seq": other}, device_id_type=pl.DeviceIdType.MESH
        )
    )

    for fetch in fetches[:4]:
        fetch.wait()
    place = []
    for aud, img in PAIRS:
        at = jnp.int32(0)
        for b in range(branches):
            f0, f1 = flags[0, b], flags[1, b]
            at = at + b * ((f0 if aud else 1 - f0) * (f1 if img else 1 - f1))
        place.append(jnp.minimum(at, branches - 1))

    def stage(h, carry):
        for p in range(branches):
            staged[h * branches + p] = video[h, place[p]]
        for p in range(0, branches, 2):
            staged_img[h * (branches // 2) + p // 2] = image[h, place[p]]
        return carry

    lax.fori_loop(0, heads, stage, 0)
    pl.semaphore_wait(barrier, n - 1)

    mine = pl.ds(pl.multiple_of(me * rows, rows), rows)
    mine_img = pl.ds(pl.multiple_of(me * img_rows, img_rows), img_rows)

    strips = n // plane
    my_strip, my_seat = me // plane, me % plane
    pltpu.sync_copy(audio_kv, gathered.at[my_seat, my_strip])

    def far(i, carry):
        strip = (my_strip + 1 + i) % strips
        send(
            audio_kv,
            gathered.at[my_seat, my_strip],
            send_a,
            recv_a,
            strip * plane + my_seat,
        )
        return carry

    lax.fori_loop(0, strips - 1, far, 0)

    def send_unit(j):
        each_peer(
            lambda other: send(
                staged.at[other * units + j], got.at[j, mine], send_v.at[j], recv_v.at[j], other
            )
        )

    def send_image(m):
        def one(other):
            if units > 1:
                item = other * (units // 2) + m
                send(staged_img.at[item], got_img.at[m, mine_img], send_i.at[m], recv_i.at[m], other)
            else:

                @pl.when(other % 2 == 0)
                def _():
                    send(
                        staged_img.at[other // 2],
                        got_img.at[m, mine_img],
                        send_i.at[m],
                        recv_i.at[m],
                        other,
                    )

        each_peer(one)

    send_unit(0)
    send_image(0)
    drain(gathered.at[0, pl.ds(0, strips - 1)], recv_a)

    def near(i, carry):
        seat = (my_seat + 1 + i) % plane
        send(
            gathered.at[my_seat], gathered.at[my_seat], send_b, recv_b, my_strip * plane + seat
        )
        return carry

    lax.fori_loop(0, plane - 1, near, 0)
    for j in range(1, units):
        send_unit(j)
        if j % 2 == 0:
            send_image(j // 2)

    for j in range(units):
        got[j, mine] = staged[me * units + j]
    if units > 1:
        for m in range(units // 2):
            got_img[m, mine_img] = staged_img[me * (units // 2) + m]
    else:

        @pl.when(me % 2 == 0)
        def _():
            got_img[0, mine_img] = staged_img[me // 2]

    for fetch in fetches[4:]:
        fetch.wait()
    spots = lax.broadcasted_iota(jnp.int32, (rows, 1), 0)

    def start_of(t, column):
        return jnp.where(spots == t, starts[frames[me * rows + t]], column)

    first = lax.fori_loop(0, rows, start_of, jnp.zeros((rows, 1), jnp.int32))
    audio_rows = audio_kv.shape[0]
    audio_count = n * audio_rows
    slots = lax.broadcasted_iota(jnp.int32, (rows, audio_count), 1)
    inside = (slots >= first) & (slots < first + AUD_WIN)
    ranks = audio_q.shape[0]
    inside = jnp.concatenate([inside] * ranks, axis=0)

    drain(gathered.at[pl.ds(0, plane - 1)], recv_b)
    per = 8 // audio_rows

    def widen(g, carry):
        pieces = []
        for i in range(per):
            src = g * per + i
            pieces.append(gathered[src % plane, src // plane].astype(jnp.float32))
        audio_wide[pl.ds(pl.multiple_of(g * 8, 8), 8), :] = jnp.concatenate(pieces, axis=0)
        return carry

    lax.fori_loop(0, audio_count // 8, widen, 0)
    scale = 1.0 / math.sqrt(dim)
    log2e = math.log2(math.e)
    transposed = (((1,), (1,)), ((), ()))

    def audio_head(h, carry):
        cols = pl.ds(pl.multiple_of(h * dim, dim), dim)
        val_cols = pl.ds(pl.multiple_of(inner + h * dim, dim), dim)
        q = audio_q[:, :, cols].reshape(ranks * rows, dim)
        k = audio_wide[:, cols].astype(jnp.bfloat16)
        v = audio_wide[:, val_cols].astype(jnp.bfloat16)
        s = lax.dot_general(q, k, transposed, preferred_element_type=jnp.float32)
        s = jnp.where(inside, s, -jnp.inf)
        top = jnp.max(s, axis=1, keepdims=True)
        w = jnp.where(inside, jnp.exp2((s - top) * (scale * log2e)), 0.0)
        total = jnp.sum(w, axis=1, keepdims=True)
        o = jnp.dot(w.astype(jnp.bfloat16), v, preferred_element_type=jnp.float32) / total
        audio_out[:, :, cols] = o.reshape(ranks, rows, dim)
        return carry

    lax.fori_loop(0, heads, audio_head, 0)

    blocks = tokens // q_block
    per_block = q_block // rows
    turn = me // per_block + 1

    def attend(j, with_image):
        def block(i, carry):
            b = (turn + i) % blocks
            at = pl.ds(pl.multiple_of(b * q_block, q_block), q_block)
            q = got[j, at, 0:dim]
            k = got[j, :, dim : 2 * dim]
            v = got[j, :, 2 * dim :]
            s = lax.dot_general(q, k, transposed, preferred_element_type=jnp.float32)
            top = jnp.max(s, axis=1, keepdims=True)
            if with_image:
                ki = got_img[j // 2, :, 0:dim]
                vi = got_img[j // 2, :, dim:]
                si = lax.dot_general(q, ki, transposed, preferred_element_type=jnp.float32)
                top = jnp.maximum(top, jnp.max(si, axis=1, keepdims=True))
            w = jnp.exp2((s - top) * (scale * log2e))
            total = jnp.sum(w, axis=1, keepdims=True)
            o = jnp.dot(w.astype(jnp.bfloat16), v, preferred_element_type=jnp.float32)
            if with_image:
                wi = jnp.exp2((si - top) * (scale * log2e))
                total = total + jnp.sum(wi, axis=1, keepdims=True)
                o = o + jnp.dot(wi.astype(jnp.bfloat16), vi, preferred_element_type=jnp.float32)
            outs[j, at, :] = (o / total).astype(jnp.bfloat16)

            def give(d, inner_carry):
                other = b * per_block + d
                part = outs.at[j, pl.ds(pl.multiple_of(other * rows, rows), rows)]

                @pl.when(other != me)
                def _():
                    send(part, back.at[j, me], send_o.at[j], recv_o.at[j], other)

                return inner_carry

            lax.fori_loop(0, per_block, give, 0)
            return carry

        lax.fori_loop(0, blocks, block, 0)
        back[j, me] = outs[j, mine, :]

    for j in range(units):
        drain(got.at[j, pl.ds(0, (n - 1) * rows)], recv_v.at[j])
        if units > 1:
            if j % 2 == 0:
                drain(got_img.at[j // 2, pl.ds(0, (n - 1) * img_rows)], recv_i.at[j // 2])
            attend(j, j % 2 == 0)
        else:

            @pl.when(me % 2 == 0)
            def _():
                drain(got_img.at[0, pl.ds(0, (n - 1) * img_rows)], recv_i.at[0])
                attend(0, True)

            @pl.when(me % 2 == 1)
            def _():
                attend(0, False)

    swapped = jnp.where(place[0] > place[1], 1, 0)
    seats = (swapped, 1 - swapped)
    result = jnp.zeros(mixed.shape, jnp.float32)
    for j in range(units):
        drain(back.at[j, pl.ds(0, n - 1)], recv_o.at[j])
        for p in range(j, branches, units):
            for h in range(heads):
                cols = slice(h * dim, (h + 1) * dim)
                x = back[j, (h * branches + p) // units].astype(jnp.float32)
                if PAIRS[p][0]:
                    x = x + audio_out[seats[p], :, cols]
                hidden[:, cols] = x
            x = hidden[...]
            center = jnp.mean(x, axis=1, keepdims=True)
            x = x - center
            spread = jnp.mean(jnp.square(x), axis=1, keepdims=True)
            x = x * lax.rsqrt(spread + 1e-06)
            gain = modulation[1, pl.ds(place[p], 1), :]
            shift = modulation[0, pl.ds(place[p], 1), :]
            x = (x * (1.0 + gain) + shift).astype(jnp.bfloat16)
            y = lax.dot_general(x, final_weight[...], transposed, preferred_element_type=jnp.float32)
            result = result + guide[place[p]].astype(jnp.float32) * y
    mixed[...] = result

    drain(gathered.at[0, pl.ds(0, strips - 1)], send_a)
    drain(gathered.at[pl.ds(0, plane - 1)], send_b)
    for j in range(units):
        drain(staged.at[pl.ds(0, n - 1)], send_v.at[j])
        drain(back.at[j, pl.ds(0, n - 1)], send_o.at[j])
    if units > 1:
        for m in range(units // 2):
            drain(staged_img.at[pl.ds(0, n - 1)], send_i.at[m])
    else:

        @pl.when(me % 2 == 0)
        def _():
            drain(staged_img.at[pl.ds(0, n // 2 - 1)], send_i.at[0])

        @pl.when(me % 2 == 1)
        def _():
            drain(staged_img.at[pl.ds(0, n // 2)], send_i.at[0])


def split_kernel(
    n,
    q_block,
    plane,
    flags_in,
    guide_in,
    frames_in,
    starts_in,
    video_in,
    image_in,
    audio_q_in,
    audio_kv_in,
    modulation_in,
    final_weight_in,
    mixed,
    flags,
    guide,
    frames,
    starts,
    video,
    image,
    audio_q,
    audio_kv,
    modulation,
    final_weight,
    loads,
    st_q,
    st_k,
    st_c,
    got_q,
    got_k,
    got_c,
    out_b,
    out_s,
    out_c,
    out_y,
    out_z,
    back_b,
    back_s,
    back_c,
    back_y,
    back_z,
    gathered,
    audio_wide,
    audio_out,
    hidden,
    weights,
    folded,
    sends,
    recvs,
    ready,
):
    heads, branches, rows, wide = video.shape
    dim = wide // 3
    img_rows = image.shape[2]
    inner = heads * dim
    half = n // 2
    quarter = n // 4
    channels = final_weight.shape[0]
    me = lax.axis_index("seq")
    loc = me % half
    bits = (n - 1).bit_length()
    flips = [(1 - 2 * ((me // 2**i) % 2)) * 2**i for i in range(bits)]

    def partner(k):
        other = me
        for i in range(bits):
            other = other + ((k // 2**i) % 2) * flips[i]
        return other

    def loop(count, body):
        def step(i, carry):
            body(i)
            return carry

        lax.fori_loop(0, count, step, 0)

    def send(src, dst, which, other):
        pltpu.make_async_remote_copy(
            src_ref=src,
            dst_ref=dst,
            send_sem=sends.at[which],
            recv_sem=recvs.at[which],
            device_id={"seq": other},
            device_id_type=pl.DeviceIdType.MESH,
        ).start()

    def drain(ref, sem):
        pltpu.make_async_copy(ref, ref, sem).wait()

    Q, K, C, FAR, NEAR, RB, RS, RC, RY, RZ = range(10)

    central = (me >= quarter) & (me < half + quarter)
    my_head = jnp.where(central, me - quarter, jnp.where(me < quarter, me, me - half))

    kin = [k for k in range(n - 1, 0, -1) if k < plane or k % plane < 2]
    rest = [k for k in range(n - 1, 0, -1) if k not in kin]

    def greet(sem):
        for k in kin:
            pl.semaphore_signal(
                sem, inc=1, device_id={"seq": partner(k)}, device_id_type=pl.DeviceIdType.MESH
            )

    barrier = pltpu.get_barrier_semaphore()
    greet(barrier)
    pairs = (
        (flags_in, flags),
        (video_in, video),
        (image_in, image),
        (audio_kv_in, audio_kv),
        (frames_in, frames),
        (starts_in, starts),
        (guide_in, guide),
        (audio_q_in, audio_q),
        (modulation_in, modulation),
        (final_weight_in, final_weight),
    )
    fetches = [pltpu.make_async_copy(src, dst, loads.at[i]) for i, (src, dst) in enumerate(pairs)]
    for fetch in fetches:
        fetch.start()
    for fetch in fetches[:4]:
        fetch.wait()
    place = []
    for aud, img in PAIRS:
        at = jnp.int32(0)
        for b in range(branches):
            f0, f1 = flags[0, b], flags[1, b]
            at = at + b * ((f0 if aud else 1 - f0) * (f1 if img else 1 - f1))
        place.append(jnp.minimum(at, branches - 1))

    def stage(h):
        for j in range(2):
            x = video[h, place[2 * j]]
            st_q[h, :, j * dim : (j + 1) * dim] = x[:, :dim]
            st_k[h, :, 2 * j * dim : 2 * (j + 1) * dim] = x[:, dim:]
            st_k[h, j * img_rows : (j + 1) * img_rows, 4 * dim :] = image[h, place[2 * j]]
        st_c[quarter + h] = video[h, place[1]]
        st_c[h + jnp.where(h < quarter, 0, half)] = video[h, place[3]]

    loop(heads, stage)
    pl.semaphore_wait(barrier, len(kin))
    greet(ready)

    strips = n // plane
    my_strip, my_seat = me // plane, me % plane
    pltpu.sync_copy(audio_kv, gathered.at[my_seat, my_strip])

    def far(i):
        strip = (my_strip + 1 + i) % strips
        send(audio_kv, gathered.at[my_seat, my_strip], FAR, strip * plane + my_seat)

    loop(strips - 1, far)

    def send_q(other):
        send(st_q.at[other % half], got_q.at[me], Q, other)

    def send_k(other):
        send(st_k.at[other % half], got_k.at[loc], K, other)

    def send_c(other):
        send(st_c.at[other], got_c.at[me], C, other)

    def mixed_order(ks):
        cross, same = [k for k in ks if k >= half], [k for k in ks if k < half]
        for i in range(max(len(cross), len(same))):
            yield from cross[i : i + 1] + same[i : i + 1]

    def first(ks):
        for k in mixed_order(ks):
            other = partner(k)
            if k < half:
                send_k(other)
            send_q(other)

    first(kin)
    pl.semaphore_wait(ready, len(kin))
    first(rest)
    drain(gathered.at[0, pl.ds(0, strips - 1)], recvs.at[FAR])

    def near(i):
        seat = (my_seat + 1 + i) % plane
        send(gathered.at[my_seat], gathered.at[my_seat], NEAR, my_strip * plane + seat)

    loop(plane - 1, near)

    def second(i):
        send_c(partner(n - 1 - i))

    loop(n - 1, second)

    got_q[me] = st_q[loc]
    got_k[loc] = st_k[loc]
    got_c[me] = st_c[me]

    scale = 1.0 / math.sqrt(dim)
    rate = scale * math.log2(math.e)
    transposed = (((1,), (1,)), ((), ()))

    blocks = n * rows // q_block
    per_block = q_block // rows
    turn = me // per_block + 1

    def attend(q, keys, values):
        scores = [lax.dot_general(q, k, transposed, preferred_element_type=jnp.float32) for k in keys]
        top = functools.reduce(jnp.maximum, [jnp.max(s, axis=1, keepdims=True) for s in scores])
        total, o = 0.0, 0.0
        for s, v in zip(scores, values):
            w = jnp.exp2((s - top) * rate)
            total = total + jnp.sum(w, axis=1, keepdims=True)
            o = o + jnp.dot(w.astype(jnp.bfloat16), v, preferred_element_type=jnp.float32)
        return (o / total).astype(jnp.bfloat16), top, total

    def give(b, body):
        def one(d):
            other = b * per_block + d

            @pl.when(other != me)
            def _():
                body(other)

        loop(per_block, one)

    for fetch in fetches[4:]:
        fetch.wait()
    drain(got_q.at[pl.ds(0, n - 1)], recvs.at[Q])
    drain(got_k.at[pl.ds(0, half - 1)], recvs.at[K])

    lane = lax.broadcasted_iota(jnp.int32, (q_block, 4 * rows), 1)
    diagonal = lane % rows == lax.broadcasted_iota(jnp.int32, (q_block, 4 * rows), 0) % rows

    head_of = lax.broadcasted_iota(jnp.int32, (folded.shape[0], inner), 1) // dim
    line = lax.broadcasted_iota(jnp.int32, (folded.shape[0], inner), 0)
    gains = 1.0 + modulation[1, pl.ds(place[3], 1), :]
    table = jnp.where(line == head_of, gains, jnp.where(line == heads, modulation[0, pl.ds(place[3], 1), :], 0.0))
    folded[...] = lax.dot_general(
        table,
        final_weight[...].astype(jnp.float32),
        transposed,
        precision=lax.Precision.HIGHEST,
        preferred_element_type=jnp.float32,
    )

    def image_block(i):
        b = (turn + i) % blocks
        devices = pl.ds(pl.multiple_of(b * per_block, per_block), per_block)
        stats = []
        for j in range(2):
            q = got_q[devices, :, j * dim : (j + 1) * dim].reshape(q_block, dim)
            at = 2 * j * dim
            k = got_k[:, :, at : at + dim].reshape(half * rows, dim)
            v = got_k[:, :, at + dim : at + 2 * dim].reshape(half * rows, dim)
            pick = slice(j * img_rows, (j + 1) * img_rows)
            ki = got_k[:, pick, 4 * dim : 5 * dim].reshape(half * img_rows, dim)
            vi = got_k[:, pick, 5 * dim :].reshape(half * img_rows, dim)
            o, top, total = attend(q, (k, ki), (v, vi))
            out_b[devices, :, j * dim : (j + 1) * dim] = o.reshape(per_block, rows, dim)
            stats += [top, total]
        x = jnp.where(lane < rows, stats[0], jnp.where(lane < 2 * rows, stats[1], jnp.where(lane < 3 * rows, stats[2], stats[3])))
        x = jnp.where(diagonal, x, 0.0).reshape(per_block, rows, 4 * rows)
        out_s[devices, 0, :] = jnp.sum(x, axis=1)

        def body(other):
            send(out_b.at[other], back_b.at[me], RB, other)
            send(out_s.at[other], back_s.at[me], RS, other)

        give(b, body)

    loop(blocks, image_block)
    back_b[me] = out_b[me]
    back_s[me] = out_s[me]

    spots = lax.broadcasted_iota(jnp.int32, (rows, 1), 0)

    def start_of(t, column):
        return jnp.where(spots == t, starts[frames[me * rows + t]], column)

    begin = lax.fori_loop(0, rows, start_of, jnp.zeros((rows, 1), jnp.int32))
    audio_rows = audio_kv.shape[0]
    audio_count = n * audio_rows
    slots = lax.broadcasted_iota(jnp.int32, (rows, audio_count), 1)
    inside = (slots >= begin) & (slots < begin + AUD_WIN)
    ranks = audio_q.shape[0]
    inside = jnp.concatenate([inside] * ranks, axis=0)

    drain(gathered.at[pl.ds(0, plane - 1)], recvs.at[NEAR])
    per = 8 // audio_rows

    def widen(g):
        pieces = []
        for i in range(per):
            src = g * per + i
            pieces.append(gathered[src % plane, src // plane].astype(jnp.float32))
        audio_wide[pl.ds(pl.multiple_of(g * 8, 8), 8), :] = jnp.concatenate(pieces, axis=0)

    loop(audio_count // 8, widen)
    def audio_head(h):
        cols = pl.ds(pl.multiple_of(h * dim, dim), dim)
        val_cols = pl.ds(pl.multiple_of(inner + h * dim, dim), dim)
        q = audio_q[:, :, cols].reshape(ranks * rows, dim)
        k = audio_wide[:, cols].astype(jnp.bfloat16)
        v = audio_wide[:, val_cols].astype(jnp.bfloat16)
        s = lax.dot_general(q, k, transposed, preferred_element_type=jnp.float32)
        s = jnp.where(inside, s, -jnp.inf)
        top = jnp.max(s, axis=1, keepdims=True)
        w = jnp.where(inside, jnp.exp2((s - top) * rate), 0.0)
        total = jnp.sum(w, axis=1, keepdims=True)
        o = jnp.dot(w.astype(jnp.bfloat16), v, preferred_element_type=jnp.float32) / total
        audio_out[:, :, cols] = o.reshape(ranks, rows, dim)

    loop(3 * heads // 4, audio_head)

    drain(got_c.at[pl.ds(0, n - 1)], recvs.at[C])

    def plain_block(i):
        b = (turn + i) % blocks
        devices = pl.ds(pl.multiple_of(b * per_block, per_block), per_block)
        q = got_c[devices, :, 0:dim].reshape(q_block, dim)
        k = got_c[:, :, dim : 2 * dim].reshape(n * rows, dim)
        v = got_c[:, :, 2 * dim :].reshape(n * rows, dim)
        o, _, _ = attend(q, (k,), (v,))

        @pl.when(central)
        def _():
            out_c[devices] = o.reshape(per_block, rows, dim)
            give(b, lambda other: send(out_c.at[other], back_c.at[my_head], RC, other))

        @pl.when(jnp.logical_not(central))
        def _():
            x = o.astype(jnp.float32)
            center = jnp.mean(x, axis=1, keepdims=True)
            x = x - center
            spread = jnp.sum(jnp.square(x), axis=1, keepdims=True)
            cols = pl.ds(pl.multiple_of(my_head * dim, dim), dim)
            chosen = lax.broadcasted_iota(jnp.int32, (branches, dim), 0) == place[3]
            gain = jnp.sum(jnp.where(chosen, modulation[1, :, cols], 0.0), axis=0, keepdims=True)
            x = (x * (1.0 + gain)).astype(jnp.bfloat16)
            y = lax.dot_general(x, final_weight[:, cols], transposed, preferred_element_type=jnp.float32)
            y = y.reshape(per_block, rows, channels)
            y = jnp.concatenate([y[:, : rows // 2], y[:, rows // 2 :]], axis=2)
            out_y[devices] = y.astype(jnp.bfloat16)
            z = jnp.where(lane < rows, center, jnp.where(lane < 2 * rows, spread, 0.0))
            z = jnp.where(diagonal, z, 0.0).reshape(per_block, rows, 4 * rows)
            out_z[devices, 0, :] = jnp.sum(z, axis=1)

            def body(other):
                send(out_y.at[other], back_y.at[my_head], RY, other)
                send(out_z.at[other], back_z.at[my_head], RZ, other)

            give(b, body)

    loop(blocks, plain_block)

    @pl.when(central)
    def _():
        back_c[my_head] = out_c[me]

    @pl.when(jnp.logical_not(central))
    def _():
        back_y[my_head] = out_y[me]
        back_z[my_head] = out_z[me]

    loop(heads - 3 * heads // 4, lambda i: audio_head(3 * heads // 4 + i))
    swapped = jnp.where(place[0] > place[1], 1, 0)
    seats = (swapped, 1 - swapped)

    def finish(p, result):
        x = hidden[...]
        center = jnp.mean(x, axis=1, keepdims=True)
        x = x - center
        spread = jnp.mean(jnp.square(x), axis=1, keepdims=True)
        x = x * lax.rsqrt(spread + 1e-06)
        gain = modulation[1, pl.ds(place[p], 1), :]
        shift = modulation[0, pl.ds(place[p], 1), :]
        x = (x * (1.0 + gain) + shift).astype(jnp.bfloat16)
        y = lax.dot_general(x, final_weight[...], transposed, preferred_element_type=jnp.float32)
        return result + guide[place[p]].astype(jnp.float32) * y

    result = jnp.zeros(mixed.shape, jnp.float32)
    drain(back_b.at[pl.ds(0, n - 1)], recvs.at[RB])
    drain(back_s.at[pl.ds(0, n - 1)], recvs.at[RS])
    a, b = back_s[0:half, 0, :], back_s[half:n, 0, :]
    most = jnp.maximum(a, b)
    lanes = 4 * rows
    a = jnp.exp2((a - most) * rate) * pltpu.roll(a, lanes - rows, 1)
    b = jnp.exp2((b - most) * rate) * pltpu.roll(b, lanes - rows, 1)
    whole = a + b
    parts = [a / whole, b / whole, jnp.zeros((lanes - n, lanes), jnp.float32)]
    weights[...] = jnp.concatenate(parts, axis=0).T
    for j in range(2):
        p = 2 * j
        tokens = slice(2 * j * rows, (2 * j + 1) * rows)
        for h in range(heads):
            cols = slice(h * dim, (h + 1) * dim)
            x = weights[tokens, h : h + 1] * back_b[h, :, j * dim : (j + 1) * dim].astype(jnp.float32)
            other = half + h
            x = x + weights[tokens, other : other + 1] * back_b[other, :, j * dim : (j + 1) * dim].astype(jnp.float32)
            if PAIRS[p][0]:
                x = x + audio_out[seats[p], :, cols]
            hidden[:, cols] = x
        result = finish(p, result)

    @pl.when(central)
    def _():
        drain(back_c.at[pl.ds(0, heads - 1)], recvs.at[RC])
        drain(back_y, recvs.at[RY])
        drain(back_z, recvs.at[RZ])

    @pl.when(jnp.logical_not(central))
    def _():
        drain(back_c, recvs.at[RC])
        drain(back_y.at[pl.ds(0, heads - 1)], recvs.at[RY])
        drain(back_z.at[pl.ds(0, heads - 1)], recvs.at[RZ])

    for h in range(heads):
        cols = slice(h * dim, (h + 1) * dim)
        hidden[:, cols] = back_c[h].astype(jnp.float32) + audio_out[seats[1], :, cols]
    result = finish(1, result)
    z = back_z[:, 0, :]
    center = jnp.mean(z, axis=0, keepdims=True)
    away = z - center
    spread = jnp.sum(pltpu.roll(z, lanes - rows, 1) + dim * jnp.square(away), axis=0, keepdims=True) / inner
    parts = [away, lax.rsqrt(spread + 1e-06), jnp.zeros((lanes - heads - 1, lanes), jnp.float32)]
    weights[...] = jnp.concatenate(parts, axis=0).T
    y = functools.reduce(jnp.add, [back_y[h].astype(jnp.float32) for h in range(heads)])
    y = jnp.concatenate([y[:, :channels], y[:, channels:]], axis=0)
    for h in range(heads):
        y = y + weights[0:rows, h : h + 1] * folded[h : h + 1, :]
    y = weights[0:rows, heads : heads + 1] * y + folded[heads : heads + 1, :]
    result = result + guide[place[3]].astype(jnp.float32) * y
    mixed[...] = result

    drain(gathered.at[0, pl.ds(0, strips - 1)], sends.at[FAR])
    drain(gathered.at[pl.ds(0, plane - 1)], sends.at[NEAR])
    drain(got_q.at[pl.ds(0, n - 1)], sends.at[Q])
    drain(got_k.at[pl.ds(0, half - 1)], sends.at[K])
    drain(got_c.at[pl.ds(0, n - 1)], sends.at[C])
    drain(back_b.at[pl.ds(0, n - 1)], sends.at[RB])
    drain(back_s.at[pl.ds(0, n - 1)], sends.at[RS])

    @pl.when(central)
    def _():
        drain(out_c.at[pl.ds(0, n - 1)], sends.at[RC])

    @pl.when(jnp.logical_not(central))
    def _():
        drain(out_y.at[pl.ds(0, n - 1)], sends.at[RY])
        drain(out_z.at[pl.ds(0, n - 1)], sends.at[RZ])


def shards(
    video_heads,
    image_heads,
    audio_queries,
    audio_keys,
    condition_flags,
    guidance_weights,
    token_frame,
    window_start,
    modulation,
    final_weight,
    noisy_latent,
):
    heads, branches, rows, wide = video_heads.shape
    dim = wide // 3
    img_rows = image_heads.shape[2]
    n = lax.axis_size("seq")
    units = heads * branches // n
    assert n & (n - 1) == 0 and units in (1, 2, 4)
    bits = (n - 1).bit_length()
    plane = 2 ** ((bits + 1) // 2)
    tokens = n * rows
    q_block = min(256, tokens)
    images = max(1, units // 2)
    inner = heads * dim
    bf16, f32 = jnp.bfloat16, jnp.float32
    dma = pltpu.SemaphoreType.DMA
    def like(x, space):
        return space(x.shape, x.dtype)

    columns = final_weight.T
    small = (condition_flags, guidance_weights, token_frame, window_start)
    large = (video_heads, image_heads, audio_queries, audio_keys, modulation, columns)
    channels = final_weight.shape[1]
    if 2 * heads == n and branches == 4 and 4 * rows == 128 and rows == 2 * img_rows and channels == 64:
        half = n // 2
        kernel = split_kernel
        working = [
            pltpu.VMEM((heads, rows, 2 * dim), bf16),
            pltpu.VMEM((heads, rows, 6 * dim), bf16),
            pltpu.VMEM((n, rows, wide), bf16),
            pltpu.VMEM((n, rows, 2 * dim), bf16),
            pltpu.VMEM((half, rows, 6 * dim), bf16),
            pltpu.VMEM((n, rows, wide), bf16),
            pltpu.VMEM((n, rows, 2 * dim), bf16),
            pltpu.VMEM((n, 1, 4 * rows), f32),
            pltpu.VMEM((n, rows, dim), bf16),
            pltpu.VMEM((n, rows // 2, 2 * channels), bf16),
            pltpu.VMEM((n, 1, 4 * rows), f32),
            pltpu.VMEM((n, rows, 2 * dim), bf16),
            pltpu.VMEM((n, 1, 4 * rows), f32),
            pltpu.VMEM((heads, rows, dim), bf16),
            pltpu.VMEM((heads, rows // 2, 2 * channels), bf16),
            pltpu.VMEM((heads, 1, 4 * rows), f32),
            pltpu.VMEM((plane, n // plane) + audio_keys.shape, bf16),
            pltpu.VMEM((n * audio_keys.shape[0], 2 * inner), f32),
            pltpu.VMEM((audio_queries.shape[0], rows, inner), f32),
            pltpu.VMEM((rows, inner), f32),
            pltpu.VMEM((4 * rows, 4 * rows), f32),
            pltpu.VMEM((-(-(heads + 1) // 8) * 8, channels), f32),
            dma((10,)),
            dma((10,)),
            pltpu.SemaphoreType.REGULAR,
        ]
    else:
        kernel = step_kernel
        working = [
            pltpu.VMEM((heads * branches, rows, wide), bf16),
            pltpu.VMEM((heads * branches // 2, img_rows, 2 * dim), bf16),
            pltpu.VMEM((units, tokens, wide), bf16),
            pltpu.VMEM((images, n * img_rows, 2 * dim), bf16),
            pltpu.VMEM((units, tokens, dim), bf16),
            pltpu.VMEM((units, n, rows, dim), bf16),
            pltpu.VMEM((plane, n // plane) + audio_keys.shape, bf16),
            pltpu.VMEM((n * audio_keys.shape[0], 2 * inner), f32),
            pltpu.VMEM((audio_queries.shape[0], rows, inner), f32),
            pltpu.VMEM((rows, inner), f32),
            dma((units,)),
            dma((units,)),
            dma((images,)),
            dma((images,)),
            dma,
            dma,
            dma,
            dma,
            dma((units,)),
            dma((units,)),
        ]
    mixed = pl.pallas_call(
        functools.partial(kernel, n, q_block, plane),
        out_shape=jax.ShapeDtypeStruct(noisy_latent.shape, f32),
        in_specs=[pl.BlockSpec(memory_space=pl.ANY)] * (len(small) + len(large)),
        out_specs=pl.BlockSpec(memory_space=pltpu.VMEM),
        scratch_shapes=[
            *[like(x, pltpu.SMEM) for x in small],
            *[like(x, pltpu.VMEM) for x in large],
            dma((len(small) + len(large),)),
            *working,
        ],
        compiler_params=pltpu.CompilerParams(
            collective_id=0, has_side_effects=True, vmem_limit_bytes=67026944
        ),
        name="avatar_step",
    )(*small, *large)
    velocity = mixed / 8.0
    return (velocity, noisy_latent - 0.125 * velocity)


def solution(mesh):
    in_specs = (
        P("groups", None, "seq", None),
        P("groups", None, "seq", None),
        P("groups", "seq", None),
        P("seq", "groups"),
        P("groups", None),
        P("groups"),
        P("groups"),
        P("groups"),
        P("groups", None, None),
        P(),
        P(("groups", "seq"), None),
    )
    out_specs = (P(("groups", "seq"), None), P(("groups", "seq"), None))
    return jax.shard_map(shards, mesh=mesh, in_specs=in_specs, out_specs=out_specs, check_vma=False)
```

```python
import functools
import math

import jax
import jax.numpy as jnp
from jax import lax
from jax.experimental import pallas as pl
from jax.experimental.pallas import tpu as pltpu
from jax.sharding import PartitionSpec as P

AUD_WIN = 32
PAIRS = ((1, 1), (1, 0), (0, 1), (0, 0))


def step_kernel(
    n,
    q_block,
    plane,
    flags_in,
    guide_in,
    frames_in,
    starts_in,
    video_in,
    image_in,
    audio_q_in,
    audio_kv_in,
    modulation_in,
    final_weight_in,
    mixed,
    flags,
    guide,
    frames,
    starts,
    video,
    image,
    audio_q,
    audio_kv,
    modulation,
    final_weight,
    loads,
    staged,
    staged_img,
    got,
    got_img,
    outs,
    back,
    gathered,
    audio_wide,
    audio_out,
    hidden,
    send_v,
    recv_v,
    send_i,
    recv_i,
    send_a,
    recv_a,
    send_b,
    recv_b,
    send_o,
    recv_o,
):
    heads, branches, rows, wide = video.shape
    dim = wide // 3
    img_rows = image.shape[2]
    inner = heads * dim
    units = heads * branches // n
    tokens = n * rows
    me = lax.axis_index("seq")
    bits = (n - 1).bit_length()
    flips = [(1 - 2 * ((me // 2**i) % 2)) * 2**i for i in range(bits)]

    def partner(k):
        other = me
        for i in range(bits):
            other = other + ((k // 2**i) % 2) * flips[i]
        return other

    def each_peer(body):
        def step(i, carry):
            body(partner(n - 1 - i))
            return carry

        lax.fori_loop(0, n - 1, step, 0)

    def send(src, dst, s_sem, r_sem, other):
        pltpu.make_async_remote_copy(
            src_ref=src,
            dst_ref=dst,
            send_sem=s_sem,
            recv_sem=r_sem,
            device_id={"seq": other},
            device_id_type=pl.DeviceIdType.MESH,
        ).start()

    def drain(ref, sem):
        pltpu.make_async_copy(ref, ref, sem).wait()

    pairs = (
        (flags_in, flags),
        (video_in, video),
        (image_in, image),
        (audio_kv_in, audio_kv),
        (frames_in, frames),
        (starts_in, starts),
        (guide_in, guide),
        (audio_q_in, audio_q),
        (modulation_in, modulation),
        (final_weight_in, final_weight),
    )
    fetches = [pltpu.make_async_copy(src, dst, loads.at[i]) for i, (src, dst) in enumerate(pairs)]
    for fetch in fetches:
        fetch.start()

    barrier = pltpu.get_barrier_semaphore()
    each_peer(
        lambda other: pl.semaphore_signal(
            barrier, inc=1, device_id={"seq": other}, device_id_type=pl.DeviceIdType.MESH
        )
    )

    for fetch in fetches[:4]:
        fetch.wait()
    place = []
    for aud, img in PAIRS:
        at = jnp.int32(0)
        for b in range(branches):
            f0, f1 = flags[0, b], flags[1, b]
            at = at + b * ((f0 if aud else 1 - f0) * (f1 if img else 1 - f1))
        place.append(jnp.minimum(at, branches - 1))

    def stage(h, carry):
        for p in range(branches):
            staged[h * branches + p] = video[h, place[p]]
        for p in range(0, branches, 2):
            staged_img[h * (branches // 2) + p // 2] = image[h, place[p]]
        return carry

    lax.fori_loop(0, heads, stage, 0)
    pl.semaphore_wait(barrier, n - 1)

    mine = pl.ds(pl.multiple_of(me * rows, rows), rows)
    mine_img = pl.ds(pl.multiple_of(me * img_rows, img_rows), img_rows)

    strips = n // plane
    my_strip, my_seat = me // plane, me % plane
    pltpu.sync_copy(audio_kv, gathered.at[my_seat, my_strip])

    def far(i, carry):
        strip = (my_strip + 1 + i) % strips
        send(
            audio_kv,
            gathered.at[my_seat, my_strip],
            send_a,
            recv_a,
            strip * plane + my_seat,
        )
        return carry

    lax.fori_loop(0, strips - 1, far, 0)

    def send_unit(j):
        each_peer(
            lambda other: send(
                staged.at[other * units + j], got.at[j, mine], send_v.at[j], recv_v.at[j], other
            )
        )

    def send_image(m):
        def one(other):
            if units > 1:
                item = other * (units // 2) + m
                send(staged_img.at[item], got_img.at[m, mine_img], send_i.at[m], recv_i.at[m], other)
            else:

                @pl.when(other % 2 == 0)
                def _():
                    send(
                        staged_img.at[other // 2],
                        got_img.at[m, mine_img],
                        send_i.at[m],
                        recv_i.at[m],
                        other,
                    )

        each_peer(one)

    send_unit(0)
    send_image(0)
    drain(gathered.at[0, pl.ds(0, strips - 1)], recv_a)

    def near(i, carry):
        seat = (my_seat + 1 + i) % plane
        send(
            gathered.at[my_seat], gathered.at[my_seat], send_b, recv_b, my_strip * plane + seat
        )
        return carry

    lax.fori_loop(0, plane - 1, near, 0)
    for j in range(1, units):
        send_unit(j)
        if j % 2 == 0:
            send_image(j // 2)

    for j in range(units):
        got[j, mine] = staged[me * units + j]
    if units > 1:
        for m in range(units // 2):
            got_img[m, mine_img] = staged_img[me * (units // 2) + m]
    else:

        @pl.when(me % 2 == 0)
        def _():
            got_img[0, mine_img] = staged_img[me // 2]

    for fetch in fetches[4:]:
        fetch.wait()
    spots = lax.broadcasted_iota(jnp.int32, (rows, 1), 0)

    def start_of(t, column):
        return jnp.where(spots == t, starts[frames[me * rows + t]], column)

    first = lax.fori_loop(0, rows, start_of, jnp.zeros((rows, 1), jnp.int32))
    audio_rows = audio_kv.shape[0]
    audio_count = n * audio_rows
    slots = lax.broadcasted_iota(jnp.int32, (rows, audio_count), 1)
    inside = (slots >= first) & (slots < first + AUD_WIN)
    ranks = audio_q.shape[0]
    inside = jnp.concatenate([inside] * ranks, axis=0)

    drain(gathered.at[pl.ds(0, plane - 1)], recv_b)
    per = 8 // audio_rows

    def widen(g, carry):
        pieces = []
        for i in range(per):
            src = g * per + i
            pieces.append(gathered[src % plane, src // plane].astype(jnp.float32))
        audio_wide[pl.ds(pl.multiple_of(g * 8, 8), 8), :] = jnp.concatenate(pieces, axis=0)
        return carry

    lax.fori_loop(0, audio_count // 8, widen, 0)
    scale = 1.0 / math.sqrt(dim)
    log2e = math.log2(math.e)
    transposed = (((1,), (1,)), ((), ()))

    def audio_head(h, carry):
        cols = pl.ds(pl.multiple_of(h * dim, dim), dim)
        val_cols = pl.ds(pl.multiple_of(inner + h * dim, dim), dim)
        q = audio_q[:, :, cols].reshape(ranks * rows, dim)
        k = audio_wide[:, cols].astype(jnp.bfloat16)
        v = audio_wide[:, val_cols].astype(jnp.bfloat16)
        s = lax.dot_general(q, k, transposed, preferred_element_type=jnp.float32)
        s = jnp.where(inside, s, -jnp.inf)
        top = jnp.max(s, axis=1, keepdims=True)
        w = jnp.where(inside, jnp.exp2((s - top) * (scale * log2e)), 0.0)
        total = jnp.sum(w, axis=1, keepdims=True)
        o = jnp.dot(w.astype(jnp.bfloat16), v, preferred_element_type=jnp.float32) / total
        audio_out[:, :, cols] = o.reshape(ranks, rows, dim)
        return carry

    lax.fori_loop(0, heads, audio_head, 0)

    blocks = tokens // q_block
    per_block = q_block // rows
    turn = me // per_block + 1

    def attend(j, with_image):
        def block(i, carry):
            b = (turn + i) % blocks
            at = pl.ds(pl.multiple_of(b * q_block, q_block), q_block)
            q = got[j, at, 0:dim]
            k = got[j, :, dim : 2 * dim]
            v = got[j, :, 2 * dim :]
            s = lax.dot_general(q, k, transposed, preferred_element_type=jnp.float32)
            top = jnp.max(s, axis=1, keepdims=True)
            if with_image:
                ki = got_img[j // 2, :, 0:dim]
                vi = got_img[j // 2, :, dim:]
                si = lax.dot_general(q, ki, transposed, preferred_element_type=jnp.float32)
                top = jnp.maximum(top, jnp.max(si, axis=1, keepdims=True))
            w = jnp.exp2((s - top) * (scale * log2e))
            total = jnp.sum(w, axis=1, keepdims=True)
            o = jnp.dot(w.astype(jnp.bfloat16), v, preferred_element_type=jnp.float32)
            if with_image:
                wi = jnp.exp2((si - top) * (scale * log2e))
                total = total + jnp.sum(wi, axis=1, keepdims=True)
                o = o + jnp.dot(wi.astype(jnp.bfloat16), vi, preferred_element_type=jnp.float32)
            outs[j, at, :] = (o / total).astype(jnp.bfloat16)

            def give(d, inner_carry):
                other = b * per_block + d
                part = outs.at[j, pl.ds(pl.multiple_of(other * rows, rows), rows)]

                @pl.when(other != me)
                def _():
                    send(part, back.at[j, me], send_o.at[j], recv_o.at[j], other)

                return inner_carry

            lax.fori_loop(0, per_block, give, 0)
            return carry

        lax.fori_loop(0, blocks, block, 0)
        back[j, me] = outs[j, mine, :]

    for j in range(units):
        drain(got.at[j, pl.ds(0, (n - 1) * rows)], recv_v.at[j])
        if units > 1:
            if j % 2 == 0:
                drain(got_img.at[j // 2, pl.ds(0, (n - 1) * img_rows)], recv_i.at[j // 2])
            attend(j, j % 2 == 0)
        else:

            @pl.when(me % 2 == 0)
            def _():
                drain(got_img.at[0, pl.ds(0, (n - 1) * img_rows)], recv_i.at[0])
                attend(0, True)

            @pl.when(me % 2 == 1)
            def _():
                attend(0, False)

    swapped = jnp.where(place[0] > place[1], 1, 0)
    seats = (swapped, 1 - swapped)
    result = jnp.zeros(mixed.shape, jnp.float32)
    for j in range(units):
        drain(back.at[j, pl.ds(0, n - 1)], recv_o.at[j])
        for p in range(j, branches, units):
            for h in range(heads):
                cols = slice(h * dim, (h + 1) * dim)
                x = back[j, (h * branches + p) // units].astype(jnp.float32)
                if PAIRS[p][0]:
                    x = x + audio_out[seats[p], :, cols]
                hidden[:, cols] = x
            x = hidden[...]
            center = jnp.mean(x, axis=1, keepdims=True)
            x = x - center
            spread = jnp.mean(jnp.square(x), axis=1, keepdims=True)
            x = x * lax.rsqrt(spread + 1e-06)
            gain = modulation[1, pl.ds(place[p], 1), :]
            shift = modulation[0, pl.ds(place[p], 1), :]
            x = (x * (1.0 + gain) + shift).astype(jnp.bfloat16)
            y = lax.dot_general(x, final_weight[...], transposed, preferred_element_type=jnp.float32)
            result = result + guide[place[p]].astype(jnp.float32) * y
    mixed[...] = result

    drain(gathered.at[0, pl.ds(0, strips - 1)], send_a)
    drain(gathered.at[pl.ds(0, plane - 1)], send_b)
    for j in range(units):
        drain(staged.at[pl.ds(0, n - 1)], send_v.at[j])
        drain(back.at[j, pl.ds(0, n - 1)], send_o.at[j])
    if units > 1:
        for m in range(units // 2):
            drain(staged_img.at[pl.ds(0, n - 1)], send_i.at[m])
    else:

        @pl.when(me % 2 == 0)
        def _():
            drain(staged_img.at[pl.ds(0, n // 2 - 1)], send_i.at[0])

        @pl.when(me % 2 == 1)
        def _():
            drain(staged_img.at[pl.ds(0, n // 2)], send_i.at[0])


def split_kernel(
    n,
    q_block,
    plane,
    flags_in,
    guide_in,
    frames_in,
    starts_in,
    video_in,
    image_in,
    audio_q_in,
    audio_kv_in,
    modulation_in,
    final_weight_in,
    mixed,
    flags,
    guide,
    frames,
    starts,
    video,
    image,
    audio_q,
    audio_kv,
    modulation,
    final_weight,
    loads,
    st_q,
    st_k,
    st_c,
    got_q,
    got_k,
    got_c,
    out_b,
    out_s,
    out_c,
    out_y,
    out_z,
    back_b,
    back_s,
    back_c,
    back_y,
    back_z,
    gathered,
    audio_wide,
    audio_out,
    hidden,
    weights,
    folded,
    sends,
    recvs,
    ready,
):
    heads, branches, rows, wide = video.shape
    dim = wide // 3
    img_rows = image.shape[2]
    inner = heads * dim
    half = n // 2
    quarter = n // 4
    channels = final_weight.shape[0]
    me = lax.axis_index("seq")
    loc = me % half
    bits = (n - 1).bit_length()
    flips = [(1 - 2 * ((me // 2**i) % 2)) * 2**i for i in range(bits)]

    def partner(k):
        other = me
        for i in range(bits):
            other = other + ((k // 2**i) % 2) * flips[i]
        return other

    def loop(count, body):
        def step(i, carry):
            body(i)
            return carry

        lax.fori_loop(0, count, step, 0)

    def send(src, dst, which, other):
        pltpu.make_async_remote_copy(
            src_ref=src,
            dst_ref=dst,
            send_sem=sends.at[which],
            recv_sem=recvs.at[which],
            device_id={"seq": other},
            device_id_type=pl.DeviceIdType.MESH,
        ).start()

    def drain(ref, sem):
        pltpu.make_async_copy(ref, ref, sem).wait()

    Q, K, C, FAR, NEAR, RB, RS, RC, RY, RZ = range(10)

    central = (me >= quarter) & (me < half + quarter)
    my_head = jnp.where(central, me - quarter, jnp.where(me < quarter, me, me - half))

    kin = [k for k in range(n - 1, 0, -1) if k < plane or k % plane < 2]
    rest = [k for k in range(n - 1, 0, -1) if k not in kin]

    def greet(sem):
        for k in kin:
            pl.semaphore_signal(
                sem, inc=1, device_id={"seq": partner(k)}, device_id_type=pl.DeviceIdType.MESH
            )

    barrier = pltpu.get_barrier_semaphore()
    greet(barrier)
    pairs = (
        (flags_in, flags),
        (video_in, video),
        (image_in, image),
        (audio_kv_in, audio_kv),
        (frames_in, frames),
        (starts_in, starts),
        (guide_in, guide),
        (audio_q_in, audio_q),
        (modulation_in, modulation),
        (final_weight_in, final_weight),
    )
    fetches = [pltpu.make_async_copy(src, dst, loads.at[i]) for i, (src, dst) in enumerate(pairs)]
    for fetch in fetches:
        fetch.start()
    for fetch in fetches[:4]:
        fetch.wait()
    place = []
    for aud, img in PAIRS:
        at = jnp.int32(0)
        for b in range(branches):
            f0, f1 = flags[0, b], flags[1, b]
            at = at + b * ((f0 if aud else 1 - f0) * (f1 if img else 1 - f1))
        place.append(jnp.minimum(at, branches - 1))

    def stage(h):
        for j in range(2):
            x = video[h, place[2 * j]]
            st_q[h, :, j * dim : (j + 1) * dim] = x[:, :dim]
            st_k[h, :, 2 * j * dim : 2 * (j + 1) * dim] = x[:, dim:]
            st_k[h, j * img_rows : (j + 1) * img_rows, 4 * dim :] = image[h, place[2 * j]]
        st_c[quarter + h] = video[h, place[1]]
        st_c[h + jnp.where(h < quarter, 0, half)] = video[h, place[3]]

    loop(heads, stage)
    pl.semaphore_wait(barrier, len(kin))
    greet(ready)

    strips = n // plane
    my_strip, my_seat = me // plane, me % plane
    pltpu.sync_copy(audio_kv, gathered.at[my_seat, my_strip])

    def far(i):
        strip = (my_strip + 1 + i) % strips
        send(audio_kv, gathered.at[my_seat, my_strip], FAR, strip * plane + my_seat)

    loop(strips - 1, far)

    def send_q(other):
        send(st_q.at[other % half], got_q.at[me], Q, other)

    def send_k(other):
        send(st_k.at[other % half], got_k.at[loc], K, other)

    def send_c(other):
        send(st_c.at[other], got_c.at[me], C, other)

    def mixed_order(ks):
        cross, same = [k for k in ks if k >= half], [k for k in ks if k < half]
        for i in range(max(len(cross), len(same))):
            yield from cross[i : i + 1] + same[i : i + 1]

    def first(ks):
        for k in mixed_order(ks):
            other = partner(k)
            if k < half:
                send_k(other)
            send_q(other)

    first(kin)
    pl.semaphore_wait(ready, len(kin))
    first(rest)
    drain(gathered.at[0, pl.ds(0, strips - 1)], recvs.at[FAR])

    def near(i):
        seat = (my_seat + 1 + i) % plane
        send(gathered.at[my_seat], gathered.at[my_seat], NEAR, my_strip * plane + seat)

    loop(plane - 1, near)

    def second(i):
        send_c(partner(n - 1 - i))

    loop(n - 1, second)

    got_q[me] = st_q[loc]
    got_k[loc] = st_k[loc]
    got_c[me] = st_c[me]

    scale = 1.0 / math.sqrt(dim)
    rate = scale * math.log2(math.e)
    transposed = (((1,), (1,)), ((), ()))

    blocks = n * rows // q_block
    per_block = q_block // rows
    turn = me // per_block + 1

    def attend(q, keys, values):
        scores = [lax.dot_general(q, k, transposed, preferred_element_type=jnp.float32) for k in keys]
        top = functools.reduce(jnp.maximum, [jnp.max(s, axis=1, keepdims=True) for s in scores])
        total, o = 0.0, 0.0
        for s, v in zip(scores, values):
            w = jnp.exp2((s - top) * rate)
            total = total + jnp.sum(w, axis=1, keepdims=True)
            o = o + jnp.dot(w.astype(jnp.bfloat16), v, preferred_element_type=jnp.float32)
        return (o / total).astype(jnp.bfloat16), top, total

    def give(b, body):
        def one(d):
            other = b * per_block + d

            @pl.when(other != me)
            def _():
                body(other)

        loop(per_block, one)

    for fetch in fetches[4:]:
        fetch.wait()
    drain(got_q.at[pl.ds(0, n - 1)], recvs.at[Q])
    drain(got_k.at[pl.ds(0, half - 1)], recvs.at[K])

    lane = lax.broadcasted_iota(jnp.int32, (q_block, 4 * rows), 1)
    diagonal = lane % rows == lax.broadcasted_iota(jnp.int32, (q_block, 4 * rows), 0) % rows

    head_of = lax.broadcasted_iota(jnp.int32, (folded.shape[0], inner), 1) // dim
    line = lax.broadcasted_iota(jnp.int32, (folded.shape[0], inner), 0)
    gains = 1.0 + modulation[1, pl.ds(place[3], 1), :]
    table = jnp.where(line == head_of, gains, jnp.where(line == heads, modulation[0, pl.ds(place[3], 1), :], 0.0))
    folded[...] = lax.dot_general(
        table,
        final_weight[...].astype(jnp.float32),
        transposed,
        precision=lax.Precision.HIGHEST,
        preferred_element_type=jnp.float32,
    )

    def image_block(i):
        b = (turn + i) % blocks
        devices = pl.ds(pl.multiple_of(b * per_block, per_block), per_block)
        stats = []
        for j in range(2):
            q = got_q[devices, :, j * dim : (j + 1) * dim].reshape(q_block, dim)
            at = 2 * j * dim
            k = got_k[:, :, at : at + dim].reshape(half * rows, dim)
            v = got_k[:, :, at + dim : at + 2 * dim].reshape(half * rows, dim)
            pick = slice(j * img_rows, (j + 1) * img_rows)
            ki = got_k[:, pick, 4 * dim : 5 * dim].reshape(half * img_rows, dim)
            vi = got_k[:, pick, 5 * dim :].reshape(half * img_rows, dim)
            o, top, total = attend(q, (k, ki), (v, vi))
            out_b[devices, :, j * dim : (j + 1) * dim] = o.reshape(per_block, rows, dim)
            stats += [top, total]
        x = jnp.where(lane < rows, stats[0], jnp.where(lane < 2 * rows, stats[1], jnp.where(lane < 3 * rows, stats[2], stats[3])))
        x = jnp.where(diagonal, x, 0.0).reshape(per_block, rows, 4 * rows)
        out_s[devices, 0, :] = jnp.sum(x, axis=1)

        def body(other):
            send(out_b.at[other], back_b.at[me], RB, other)
            send(out_s.at[other], back_s.at[me], RS, other)

        give(b, body)

    loop(blocks, image_block)
    back_b[me] = out_b[me]
    back_s[me] = out_s[me]

    spots = lax.broadcasted_iota(jnp.int32, (rows, 1), 0)

    def start_of(t, column):
        return jnp.where(spots == t, starts[frames[me * rows + t]], column)

    begin = lax.fori_loop(0, rows, start_of, jnp.zeros((rows, 1), jnp.int32))
    audio_rows = audio_kv.shape[0]
    audio_count = n * audio_rows
    slots = lax.broadcasted_iota(jnp.int32, (rows, audio_count), 1)
    inside = (slots >= begin) & (slots < begin + AUD_WIN)
    ranks = audio_q.shape[0]
    inside = jnp.concatenate([inside] * ranks, axis=0)

    drain(gathered.at[pl.ds(0, plane - 1)], recvs.at[NEAR])
    per = 8 // audio_rows

    def widen(g):
        pieces = []
        for i in range(per):
            src = g * per + i
            pieces.append(gathered[src % plane, src // plane].astype(jnp.float32))
        audio_wide[pl.ds(pl.multiple_of(g * 8, 8), 8), :] = jnp.concatenate(pieces, axis=0)

    loop(audio_count // 8, widen)
    def audio_head(h):
        cols = pl.ds(pl.multiple_of(h * dim, dim), dim)
        val_cols = pl.ds(pl.multiple_of(inner + h * dim, dim), dim)
        q = audio_q[:, :, cols].reshape(ranks * rows, dim)
        k = audio_wide[:, cols].astype(jnp.bfloat16)
        v = audio_wide[:, val_cols].astype(jnp.bfloat16)
        s = lax.dot_general(q, k, transposed, preferred_element_type=jnp.float32)
        s = jnp.where(inside, s, -jnp.inf)
        top = jnp.max(s, axis=1, keepdims=True)
        w = jnp.where(inside, jnp.exp2((s - top) * rate), 0.0)
        total = jnp.sum(w, axis=1, keepdims=True)
        o = jnp.dot(w.astype(jnp.bfloat16), v, preferred_element_type=jnp.float32) / total
        audio_out[:, :, cols] = o.reshape(ranks, rows, dim)

    loop(3 * heads // 4, audio_head)

    drain(got_c.at[pl.ds(0, n - 1)], recvs.at[C])

    def plain_block(i):
        b = (me // per_block + i) % blocks
        devices = pl.ds(pl.multiple_of(b * per_block, per_block), per_block)
        q = got_c[devices, :, 0:dim].reshape(q_block, dim)
        k = got_c[:, :, dim : 2 * dim].reshape(n * rows, dim)
        v = got_c[:, :, 2 * dim :].reshape(n * rows, dim)
        o, _, _ = attend(q, (k,), (v,))

        @pl.when(central)
        def _():
            out_c[devices] = o.reshape(per_block, rows, dim)
            give(b, lambda other: send(out_c.at[other], back_c.at[my_head], RC, other))

        @pl.when(jnp.logical_not(central))
        def _():
            x = o.astype(jnp.float32)
            center = jnp.mean(x, axis=1, keepdims=True)
            x = x - center
            spread = jnp.sum(jnp.square(x), axis=1, keepdims=True)
            cols = pl.ds(pl.multiple_of(my_head * dim, dim), dim)
            chosen = lax.broadcasted_iota(jnp.int32, (branches, dim), 0) == place[3]
            gain = jnp.sum(jnp.where(chosen, modulation[1, :, cols], 0.0), axis=0, keepdims=True)
            x = (x * (1.0 + gain)).astype(jnp.bfloat16)
            y = lax.dot_general(x, final_weight[:, cols], transposed, preferred_element_type=jnp.float32)
            y = y.reshape(per_block, rows, channels)
            y = jnp.concatenate([y[:, : rows // 2], y[:, rows // 2 :]], axis=2)
            out_y[devices] = y.astype(jnp.bfloat16)
            z = jnp.where(lane < rows, center, jnp.where(lane < 2 * rows, spread, 0.0))
            z = jnp.where(diagonal, z, 0.0).reshape(per_block, rows, 4 * rows)
            out_z[devices, 0, :] = jnp.sum(z, axis=1)

            def body(other):
                send(out_y.at[other], back_y.at[my_head], RY, other)
                send(out_z.at[other], back_z.at[my_head], RZ, other)

            give(b, body)

    loop(blocks, plain_block)

    @pl.when(central)
    def _():
        back_c[my_head] = out_c[me]

    @pl.when(jnp.logical_not(central))
    def _():
        back_y[my_head] = out_y[me]
        back_z[my_head] = out_z[me]

    loop(heads - 3 * heads // 4, lambda i: audio_head(3 * heads // 4 + i))
    swapped = jnp.where(place[0] > place[1], 1, 0)
    seats = (swapped, 1 - swapped)

    def finish(p, result):
        x = hidden[...]
        center = jnp.mean(x, axis=1, keepdims=True)
        x = x - center
        spread = jnp.mean(jnp.square(x), axis=1, keepdims=True)
        x = x * lax.rsqrt(spread + 1e-06)
        gain = modulation[1, pl.ds(place[p], 1), :]
        shift = modulation[0, pl.ds(place[p], 1), :]
        x = (x * (1.0 + gain) + shift).astype(jnp.bfloat16)
        y = lax.dot_general(x, final_weight[...], transposed, preferred_element_type=jnp.float32)
        return result + guide[place[p]].astype(jnp.float32) * y

    result = jnp.zeros(mixed.shape, jnp.float32)
    drain(back_b.at[pl.ds(0, n - 1)], recvs.at[RB])
    drain(back_s.at[pl.ds(0, n - 1)], recvs.at[RS])
    a, b = back_s[0:half, 0, :], back_s[half:n, 0, :]
    most = jnp.maximum(a, b)
    lanes = 4 * rows
    a = jnp.exp2((a - most) * rate) * pltpu.roll(a, lanes - rows, 1)
    b = jnp.exp2((b - most) * rate) * pltpu.roll(b, lanes - rows, 1)
    whole = a + b
    parts = [a / whole, b / whole, jnp.zeros((lanes - n, lanes), jnp.float32)]
    weights[...] = jnp.concatenate(parts, axis=0).T
    for j in range(2):
        p = 2 * j
        tokens = slice(2 * j * rows, (2 * j + 1) * rows)
        for h in range(heads):
            cols = slice(h * dim, (h + 1) * dim)
            x = weights[tokens, h : h + 1] * back_b[h, :, j * dim : (j + 1) * dim].astype(jnp.float32)
            other = half + h
            x = x + weights[tokens, other : other + 1] * back_b[other, :, j * dim : (j + 1) * dim].astype(jnp.float32)
            if PAIRS[p][0]:
                x = x + audio_out[seats[p], :, cols]
            hidden[:, cols] = x
        result = finish(p, result)

    @pl.when(central)
    def _():
        drain(back_c.at[pl.ds(0, heads - 1)], recvs.at[RC])
        drain(back_y, recvs.at[RY])
        drain(back_z, recvs.at[RZ])

    @pl.when(jnp.logical_not(central))
    def _():
        drain(back_c, recvs.at[RC])
        drain(back_y.at[pl.ds(0, heads - 1)], recvs.at[RY])
        drain(back_z.at[pl.ds(0, heads - 1)], recvs.at[RZ])

    for h in range(heads):
        cols = slice(h * dim, (h + 1) * dim)
        hidden[:, cols] = back_c[h].astype(jnp.float32) + audio_out[seats[1], :, cols]
    result = finish(1, result)
    z = back_z[:, 0, :]
    center = jnp.mean(z, axis=0, keepdims=True)
    away = z - center
    spread = jnp.sum(pltpu.roll(z, lanes - rows, 1) + dim * jnp.square(away), axis=0, keepdims=True) / inner
    parts = [away, lax.rsqrt(spread + 1e-06), jnp.zeros((lanes - heads - 1, lanes), jnp.float32)]
    weights[...] = jnp.concatenate(parts, axis=0).T
    y = functools.reduce(jnp.add, [back_y[h].astype(jnp.float32) for h in range(heads)])
    y = jnp.concatenate([y[:, :channels], y[:, channels:]], axis=0)
    for h in range(heads):
        y = y + weights[0:rows, h : h + 1] * folded[h : h + 1, :]
    y = weights[0:rows, heads : heads + 1] * y + folded[heads : heads + 1, :]
    result = result + guide[place[3]].astype(jnp.float32) * y
    mixed[...] = result

    drain(gathered.at[0, pl.ds(0, strips - 1)], sends.at[FAR])
    drain(gathered.at[pl.ds(0, plane - 1)], sends.at[NEAR])
    drain(got_q.at[pl.ds(0, n - 1)], sends.at[Q])
    drain(got_k.at[pl.ds(0, half - 1)], sends.at[K])
    drain(got_c.at[pl.ds(0, n - 1)], sends.at[C])
    drain(back_b.at[pl.ds(0, n - 1)], sends.at[RB])
    drain(back_s.at[pl.ds(0, n - 1)], sends.at[RS])

    @pl.when(central)
    def _():
        drain(out_c.at[pl.ds(0, n - 1)], sends.at[RC])

    @pl.when(jnp.logical_not(central))
    def _():
        drain(out_y.at[pl.ds(0, n - 1)], sends.at[RY])
        drain(out_z.at[pl.ds(0, n - 1)], sends.at[RZ])


def shards(
    video_heads,
    image_heads,
    audio_queries,
    audio_keys,
    condition_flags,
    guidance_weights,
    token_frame,
    window_start,
    modulation,
    final_weight,
    noisy_latent,
):
    heads, branches, rows, wide = video_heads.shape
    dim = wide // 3
    img_rows = image_heads.shape[2]
    n = lax.axis_size("seq")
    units = heads * branches // n
    assert n & (n - 1) == 0 and units in (1, 2, 4)
    bits = (n - 1).bit_length()
    plane = 2 ** ((bits + 1) // 2)
    tokens = n * rows
    q_block = min(256, tokens)
    images = max(1, units // 2)
    inner = heads * dim
    bf16, f32 = jnp.bfloat16, jnp.float32
    dma = pltpu.SemaphoreType.DMA
    def like(x, space):
        return space(x.shape, x.dtype)

    columns = final_weight.T
    small = (condition_flags, guidance_weights, token_frame, window_start)
    large = (video_heads, image_heads, audio_queries, audio_keys, modulation, columns)
    channels = final_weight.shape[1]
    if 2 * heads == n and branches == 4 and 4 * rows == 128 and rows == 2 * img_rows and channels == 64:
        half = n // 2
        kernel = split_kernel
        working = [
            pltpu.VMEM((heads, rows, 2 * dim), bf16),
            pltpu.VMEM((heads, rows, 6 * dim), bf16),
            pltpu.VMEM((n, rows, wide), bf16),
            pltpu.VMEM((n, rows, 2 * dim), bf16),
            pltpu.VMEM((half, rows, 6 * dim), bf16),
            pltpu.VMEM((n, rows, wide), bf16),
            pltpu.VMEM((n, rows, 2 * dim), bf16),
            pltpu.VMEM((n, 1, 4 * rows), f32),
            pltpu.VMEM((n, rows, dim), bf16),
            pltpu.VMEM((n, rows // 2, 2 * channels), bf16),
            pltpu.VMEM((n, 1, 4 * rows), f32),
            pltpu.VMEM((n, rows, 2 * dim), bf16),
            pltpu.VMEM((n, 1, 4 * rows), f32),
            pltpu.VMEM((heads, rows, dim), bf16),
            pltpu.VMEM((heads, rows // 2, 2 * channels), bf16),
            pltpu.VMEM((heads, 1, 4 * rows), f32),
            pltpu.VMEM((plane, n // plane) + audio_keys.shape, bf16),
            pltpu.VMEM((n * audio_keys.shape[0], 2 * inner), f32),
            pltpu.VMEM((audio_queries.shape[0], rows, inner), f32),
            pltpu.VMEM((rows, inner), f32),
            pltpu.VMEM((4 * rows, 4 * rows), f32),
            pltpu.VMEM((-(-(heads + 1) // 8) * 8, channels), f32),
            dma((10,)),
            dma((10,)),
            pltpu.SemaphoreType.REGULAR,
        ]
    else:
        kernel = step_kernel
        working = [
            pltpu.VMEM((heads * branches, rows, wide), bf16),
            pltpu.VMEM((heads * branches // 2, img_rows, 2 * dim), bf16),
            pltpu.VMEM((units, tokens, wide), bf16),
            pltpu.VMEM((images, n * img_rows, 2 * dim), bf16),
            pltpu.VMEM((units, tokens, dim), bf16),
            pltpu.VMEM((units, n, rows, dim), bf16),
            pltpu.VMEM((plane, n // plane) + audio_keys.shape, bf16),
            pltpu.VMEM((n * audio_keys.shape[0], 2 * inner), f32),
            pltpu.VMEM((audio_queries.shape[0], rows, inner), f32),
            pltpu.VMEM((rows, inner), f32),
            dma((units,)),
            dma((units,)),
            dma((images,)),
            dma((images,)),
            dma,
            dma,
            dma,
            dma,
            dma((units,)),
            dma((units,)),
        ]
    mixed = pl.pallas_call(
        functools.partial(kernel, n, q_block, plane),
        out_shape=jax.ShapeDtypeStruct(noisy_latent.shape, f32),
        in_specs=[pl.BlockSpec(memory_space=pl.ANY)] * (len(small) + len(large)),
        out_specs=pl.BlockSpec(memory_space=pltpu.VMEM),
        scratch_shapes=[
            *[like(x, pltpu.SMEM) for x in small],
            *[like(x, pltpu.VMEM) for x in large],
            dma((len(small) + len(large),)),
            *working,
        ],
        compiler_params=pltpu.CompilerParams(
            collective_id=0, has_side_effects=True, vmem_limit_bytes=67026944
        ),
        name="avatar_step",
    )(*small, *large)
    velocity = mixed / 8.0
    return (velocity, noisy_latent - 0.125 * velocity)


def solution(mesh):
    in_specs = (
        P("groups", None, "seq", None),
        P("groups", None, "seq", None),
        P("groups", "seq", None),
        P("seq", "groups"),
        P("groups", None),
        P("groups"),
        P("groups"),
        P("groups"),
        P("groups", None, None),
        P(),
        P(("groups", "seq"), None),
    )
    out_specs = (P(("groups", "seq"), None), P(("groups", "seq"), None))
    return jax.shard_map(shards, mesh=mesh, in_specs=in_specs, out_specs=out_specs, check_vma=False)
```

```python
import functools
import math

import jax
import jax.numpy as jnp
from jax import lax
from jax.experimental import pallas as pl
from jax.experimental.pallas import tpu as pltpu
from jax.sharding import PartitionSpec as P

AUD_WIN = 32
PAIRS = ((1, 1), (1, 0), (0, 1), (0, 0))


def step_kernel(
    n,
    q_block,
    plane,
    flags_in,
    guide_in,
    frames_in,
    starts_in,
    video_in,
    image_in,
    audio_q_in,
    audio_kv_in,
    modulation_in,
    final_weight_in,
    mixed,
    flags,
    guide,
    frames,
    starts,
    video,
    image,
    audio_q,
    audio_kv,
    modulation,
    final_weight,
    loads,
    staged,
    staged_img,
    got,
    got_img,
    outs,
    back,
    gathered,
    audio_wide,
    audio_out,
    hidden,
    send_v,
    recv_v,
    send_i,
    recv_i,
    send_a,
    recv_a,
    send_b,
    recv_b,
    send_o,
    recv_o,
):
    heads, branches, rows, wide = video.shape
    dim = wide // 3
    img_rows = image.shape[2]
    inner = heads * dim
    units = heads * branches // n
    tokens = n * rows
    me = lax.axis_index("seq")
    bits = (n - 1).bit_length()
    flips = [(1 - 2 * ((me // 2**i) % 2)) * 2**i for i in range(bits)]

    def partner(k):
        other = me
        for i in range(bits):
            other = other + ((k // 2**i) % 2) * flips[i]
        return other

    def each_peer(body):
        def step(i, carry):
            body(partner(n - 1 - i))
            return carry

        lax.fori_loop(0, n - 1, step, 0)

    def send(src, dst, s_sem, r_sem, other):
        pltpu.make_async_remote_copy(
            src_ref=src,
            dst_ref=dst,
            send_sem=s_sem,
            recv_sem=r_sem,
            device_id={"seq": other},
            device_id_type=pl.DeviceIdType.MESH,
        ).start()

    def drain(ref, sem):
        pltpu.make_async_copy(ref, ref, sem).wait()

    pairs = (
        (flags_in, flags),
        (video_in, video),
        (image_in, image),
        (audio_kv_in, audio_kv),
        (frames_in, frames),
        (starts_in, starts),
        (guide_in, guide),
        (audio_q_in, audio_q),
        (modulation_in, modulation),
        (final_weight_in, final_weight),
    )
    fetches = [pltpu.make_async_copy(src, dst, loads.at[i]) for i, (src, dst) in enumerate(pairs)]
    for fetch in fetches:
        fetch.start()

    barrier = pltpu.get_barrier_semaphore()
    each_peer(
        lambda other: pl.semaphore_signal(
            barrier, inc=1, device_id={"seq": other}, device_id_type=pl.DeviceIdType.MESH
        )
    )

    for fetch in fetches[:4]:
        fetch.wait()
    place = []
    for aud, img in PAIRS:
        at = jnp.int32(0)
        for b in range(branches):
            f0, f1 = flags[0, b], flags[1, b]
            at = at + b * ((f0 if aud else 1 - f0) * (f1 if img else 1 - f1))
        place.append(jnp.minimum(at, branches - 1))

    def stage(h, carry):
        for p in range(branches):
            staged[h * branches + p] = video[h, place[p]]
        for p in range(0, branches, 2):
            staged_img[h * (branches // 2) + p // 2] = image[h, place[p]]
        return carry

    lax.fori_loop(0, heads, stage, 0)
    pl.semaphore_wait(barrier, n - 1)

    mine = pl.ds(pl.multiple_of(me * rows, rows), rows)
    mine_img = pl.ds(pl.multiple_of(me * img_rows, img_rows), img_rows)

    strips = n // plane
    my_strip, my_seat = me // plane, me % plane
    pltpu.sync_copy(audio_kv, gathered.at[my_seat, my_strip])

    def far(i, carry):
        strip = (my_strip + 1 + i) % strips
        send(
            audio_kv,
            gathered.at[my_seat, my_strip],
            send_a,
            recv_a,
            strip * plane + my_seat,
        )
        return carry

    lax.fori_loop(0, strips - 1, far, 0)

    def send_unit(j):
        each_peer(
            lambda other: send(
                staged.at[other * units + j], got.at[j, mine], send_v.at[j], recv_v.at[j], other
            )
        )

    def send_image(m):
        def one(other):
            if units > 1:
                item = other * (units // 2) + m
                send(staged_img.at[item], got_img.at[m, mine_img], send_i.at[m], recv_i.at[m], other)
            else:

                @pl.when(other % 2 == 0)
                def _():
                    send(
                        staged_img.at[other // 2],
                        got_img.at[m, mine_img],
                        send_i.at[m],
                        recv_i.at[m],
                        other,
                    )

        each_peer(one)

    send_unit(0)
    send_image(0)
    drain(gathered.at[0, pl.ds(0, strips - 1)], recv_a)

    def near(i, carry):
        seat = (my_seat + 1 + i) % plane
        send(
            gathered.at[my_seat], gathered.at[my_seat], send_b, recv_b, my_strip * plane + seat
        )
        return carry

    lax.fori_loop(0, plane - 1, near, 0)
    for j in range(1, units):
        send_unit(j)
        if j % 2 == 0:
            send_image(j // 2)

    for j in range(units):
        got[j, mine] = staged[me * units + j]
    if units > 1:
        for m in range(units // 2):
            got_img[m, mine_img] = staged_img[me * (units // 2) + m]
    else:

        @pl.when(me % 2 == 0)
        def _():
            got_img[0, mine_img] = staged_img[me // 2]

    for fetch in fetches[4:]:
        fetch.wait()
    spots = lax.broadcasted_iota(jnp.int32, (rows, 1), 0)

    def start_of(t, column):
        return jnp.where(spots == t, starts[frames[me * rows + t]], column)

    first = lax.fori_loop(0, rows, start_of, jnp.zeros((rows, 1), jnp.int32))
    audio_rows = audio_kv.shape[0]
    audio_count = n * audio_rows
    slots = lax.broadcasted_iota(jnp.int32, (rows, audio_count), 1)
    inside = (slots >= first) & (slots < first + AUD_WIN)
    ranks = audio_q.shape[0]
    inside = jnp.concatenate([inside] * ranks, axis=0)

    drain(gathered.at[pl.ds(0, plane - 1)], recv_b)
    per = 8 // audio_rows

    def widen(g, carry):
        pieces = []
        for i in range(per):
            src = g * per + i
            pieces.append(gathered[src % plane, src // plane].astype(jnp.float32))
        audio_wide[pl.ds(pl.multiple_of(g * 8, 8), 8), :] = jnp.concatenate(pieces, axis=0)
        return carry

    lax.fori_loop(0, audio_count // 8, widen, 0)
    scale = 1.0 / math.sqrt(dim)
    log2e = math.log2(math.e)
    transposed = (((1,), (1,)), ((), ()))

    def audio_head(h, carry):
        cols = pl.ds(pl.multiple_of(h * dim, dim), dim)
        val_cols = pl.ds(pl.multiple_of(inner + h * dim, dim), dim)
        q = audio_q[:, :, cols].reshape(ranks * rows, dim)
        k = audio_wide[:, cols].astype(jnp.bfloat16)
        v = audio_wide[:, val_cols].astype(jnp.bfloat16)
        s = lax.dot_general(q, k, transposed, preferred_element_type=jnp.float32)
        s = jnp.where(inside, s, -jnp.inf)
        top = jnp.max(s, axis=1, keepdims=True)
        w = jnp.where(inside, jnp.exp2((s - top) * (scale * log2e)), 0.0)
        total = jnp.sum(w, axis=1, keepdims=True)
        o = jnp.dot(w.astype(jnp.bfloat16), v, preferred_element_type=jnp.float32) / total
        audio_out[:, :, cols] = o.reshape(ranks, rows, dim)
        return carry

    lax.fori_loop(0, heads, audio_head, 0)

    blocks = tokens // q_block
    per_block = q_block // rows
    turn = me // per_block + 1

    def attend(j, with_image):
        def block(i, carry):
            b = (turn + i) % blocks
            at = pl.ds(pl.multiple_of(b * q_block, q_block), q_block)
            q = got[j, at, 0:dim]
            k = got[j, :, dim : 2 * dim]
            v = got[j, :, 2 * dim :]
            s = lax.dot_general(q, k, transposed, preferred_element_type=jnp.float32)
            top = jnp.max(s, axis=1, keepdims=True)
            if with_image:
                ki = got_img[j // 2, :, 0:dim]
                vi = got_img[j // 2, :, dim:]
                si = lax.dot_general(q, ki, transposed, preferred_element_type=jnp.float32)
                top = jnp.maximum(top, jnp.max(si, axis=1, keepdims=True))
            w = jnp.exp2((s - top) * (scale * log2e))
            total = jnp.sum(w, axis=1, keepdims=True)
            o = jnp.dot(w.astype(jnp.bfloat16), v, preferred_element_type=jnp.float32)
            if with_image:
                wi = jnp.exp2((si - top) * (scale * log2e))
                total = total + jnp.sum(wi, axis=1, keepdims=True)
                o = o + jnp.dot(wi.astype(jnp.bfloat16), vi, preferred_element_type=jnp.float32)
            outs[j, at, :] = (o / total).astype(jnp.bfloat16)

            def give(d, inner_carry):
                other = b * per_block + d
                part = outs.at[j, pl.ds(pl.multiple_of(other * rows, rows), rows)]

                @pl.when(other != me)
                def _():
                    send(part, back.at[j, me], send_o.at[j], recv_o.at[j], other)

                return inner_carry

            lax.fori_loop(0, per_block, give, 0)
            return carry

        lax.fori_loop(0, blocks, block, 0)
        back[j, me] = outs[j, mine, :]

    for j in range(units):
        drain(got.at[j, pl.ds(0, (n - 1) * rows)], recv_v.at[j])
        if units > 1:
            if j % 2 == 0:
                drain(got_img.at[j // 2, pl.ds(0, (n - 1) * img_rows)], recv_i.at[j // 2])
            attend(j, j % 2 == 0)
        else:

            @pl.when(me % 2 == 0)
            def _():
                drain(got_img.at[0, pl.ds(0, (n - 1) * img_rows)], recv_i.at[0])
                attend(0, True)

            @pl.when(me % 2 == 1)
            def _():
                attend(0, False)

    swapped = jnp.where(place[0] > place[1], 1, 0)
    seats = (swapped, 1 - swapped)
    result = jnp.zeros(mixed.shape, jnp.float32)
    for j in range(units):
        drain(back.at[j, pl.ds(0, n - 1)], recv_o.at[j])
        for p in range(j, branches, units):
            for h in range(heads):
                cols = slice(h * dim, (h + 1) * dim)
                x = back[j, (h * branches + p) // units].astype(jnp.float32)
                if PAIRS[p][0]:
                    x = x + audio_out[seats[p], :, cols]
                hidden[:, cols] = x
            x = hidden[...]
            center = jnp.mean(x, axis=1, keepdims=True)
            x = x - center
            spread = jnp.mean(jnp.square(x), axis=1, keepdims=True)
            x = x * lax.rsqrt(spread + 1e-06)
            gain = modulation[1, pl.ds(place[p], 1), :]
            shift = modulation[0, pl.ds(place[p], 1), :]
            x = (x * (1.0 + gain) + shift).astype(jnp.bfloat16)
            y = lax.dot_general(x, final_weight[...], transposed, preferred_element_type=jnp.float32)
            result = result + guide[place[p]].astype(jnp.float32) * y
    mixed[...] = result

    drain(gathered.at[0, pl.ds(0, strips - 1)], send_a)
    drain(gathered.at[pl.ds(0, plane - 1)], send_b)
    for j in range(units):
        drain(staged.at[pl.ds(0, n - 1)], send_v.at[j])
        drain(back.at[j, pl.ds(0, n - 1)], send_o.at[j])
    if units > 1:
        for m in range(units // 2):
            drain(staged_img.at[pl.ds(0, n - 1)], send_i.at[m])
    else:

        @pl.when(me % 2 == 0)
        def _():
            drain(staged_img.at[pl.ds(0, n // 2 - 1)], send_i.at[0])

        @pl.when(me % 2 == 1)
        def _():
            drain(staged_img.at[pl.ds(0, n // 2)], send_i.at[0])


def split_kernel(
    n,
    q_block,
    plane,
    flags_in,
    guide_in,
    frames_in,
    starts_in,
    video_in,
    image_in,
    audio_q_in,
    audio_kv_in,
    modulation_in,
    final_weight_in,
    mixed,
    flags,
    guide,
    frames,
    starts,
    video,
    image,
    audio_q,
    audio_kv,
    modulation,
    final_weight,
    loads,
    st_q,
    st_k,
    st_c,
    got_q,
    got_k,
    got_c,
    out_b,
    out_s,
    out_c,
    out_y,
    out_z,
    back_b,
    back_s,
    back_c,
    back_y,
    back_z,
    gathered,
    audio_wide,
    audio_out,
    hidden,
    weights,
    folded,
    sends,
    recvs,
    ready,
):
    heads, branches, rows, wide = video.shape
    dim = wide // 3
    img_rows = image.shape[2]
    inner = heads * dim
    half = n // 2
    quarter = n // 4
    channels = final_weight.shape[0]
    me = lax.axis_index("seq")
    loc = me % half
    bits = (n - 1).bit_length()
    flips = [(1 - 2 * ((me // 2**i) % 2)) * 2**i for i in range(bits)]

    def partner(k):
        other = me
        for i in range(bits):
            other = other + ((k // 2**i) % 2) * flips[i]
        return other

    def loop(count, body):
        def step(i, carry):
            body(i)
            return carry

        lax.fori_loop(0, count, step, 0)

    def send(src, dst, which, other):
        pltpu.make_async_remote_copy(
            src_ref=src,
            dst_ref=dst,
            send_sem=sends.at[which],
            recv_sem=recvs.at[which],
            device_id={"seq": other},
            device_id_type=pl.DeviceIdType.MESH,
        ).start()

    def drain(ref, sem):
        pltpu.make_async_copy(ref, ref, sem).wait()

    Q, K, C, FAR, NEAR, RB, RS, RC, RY, RZ = range(10)

    central = (me >= quarter) & (me < half + quarter)
    my_head = jnp.where(central, me - quarter, jnp.where(me < quarter, me, me - half))

    kin = [k for k in range(n - 1, 0, -1) if k < plane or k % plane < 2]
    rest = [k for k in range(n - 1, 0, -1) if k not in kin]

    def greet(sem):
        for k in kin:
            pl.semaphore_signal(
                sem, inc=1, device_id={"seq": partner(k)}, device_id_type=pl.DeviceIdType.MESH
            )

    barrier = pltpu.get_barrier_semaphore()
    greet(barrier)
    pairs = (
        (flags_in, flags),
        (video_in, video),
        (image_in, image),
        (audio_kv_in, audio_kv),
        (frames_in, frames),
        (starts_in, starts),
        (guide_in, guide),
        (audio_q_in, audio_q),
        (modulation_in, modulation),
        (final_weight_in, final_weight),
    )
    fetches = [pltpu.make_async_copy(src, dst, loads.at[i]) for i, (src, dst) in enumerate(pairs)]
    for fetch in fetches:
        fetch.start()
    for fetch in fetches[:4]:
        fetch.wait()
    place = []
    for aud, img in PAIRS:
        at = jnp.int32(0)
        for b in range(branches):
            f0, f1 = flags[0, b], flags[1, b]
            at = at + b * ((f0 if aud else 1 - f0) * (f1 if img else 1 - f1))
        place.append(jnp.minimum(at, branches - 1))

    def stage(h):
        for j in range(2):
            x = video[h, place[2 * j]]
            st_q[h, :, j * dim : (j + 1) * dim] = x[:, :dim]
            st_k[h, :, 2 * j * dim : 2 * (j + 1) * dim] = x[:, dim:]
            st_k[h, j * img_rows : (j + 1) * img_rows, 4 * dim :] = image[h, place[2 * j]]
        st_c[quarter + h] = video[h, place[1]]
        st_c[h + jnp.where(h < quarter, 0, half)] = video[h, place[3]]

    loop(heads, stage)
    pl.semaphore_wait(barrier, len(kin))
    greet(ready)

    strips = n // plane
    my_strip, my_seat = me // plane, me % plane
    pltpu.sync_copy(audio_kv, gathered.at[my_seat, my_strip])

    def far(i):
        strip = (my_strip + 1 + i) % strips
        send(audio_kv, gathered.at[my_seat, my_strip], FAR, strip * plane + my_seat)

    loop(strips - 1, far)

    def send_q(other):
        send(st_q.at[other % half], got_q.at[me], Q, other)

    def send_k(other):
        send(st_k.at[other % half], got_k.at[loc], K, other)

    def send_c(other):
        send(st_c.at[other], got_c.at[me], C, other)

    def mixed_order(ks):
        cross, same = [k for k in ks if k >= half], [k for k in ks if k < half]
        for i in range(max(len(cross), len(same))):
            yield from cross[i : i + 1] + same[i : i + 1]

    def first(ks):
        for k in mixed_order(ks):
            other = partner(k)
            if k < half:
                send_k(other)
            send_q(other)

    first(kin)
    pl.semaphore_wait(ready, len(kin))
    first(rest)
    drain(gathered.at[0, pl.ds(0, strips - 1)], recvs.at[FAR])

    def near(i):
        seat = (my_seat + 1 + i) % plane
        send(gathered.at[my_seat], gathered.at[my_seat], NEAR, my_strip * plane + seat)

    loop(plane - 1, near)

    def second(i):
        send_c(partner(n - 1 - i))

    loop(n - 1, second)

    got_q[me] = st_q[loc]
    got_k[loc] = st_k[loc]
    got_c[me] = st_c[me]

    scale = 1.0 / math.sqrt(dim)
    rate = scale * math.log2(math.e)
    transposed = (((1,), (1,)), ((), ()))

    blocks = n * rows // q_block
    per_block = q_block // rows
    turn = me // per_block + 1

    def attend(q, keys, values):
        scores = [lax.dot_general(q, k, transposed, preferred_element_type=jnp.float32) for k in keys]
        top = functools.reduce(jnp.maximum, [jnp.max(s, axis=1, keepdims=True) for s in scores])
        total, o = 0.0, 0.0
        for s, v in zip(scores, values):
            w = jnp.exp2((s - top) * rate)
            total = total + jnp.sum(w, axis=1, keepdims=True)
            o = o + jnp.dot(w.astype(jnp.bfloat16), v, preferred_element_type=jnp.float32)
        return (o / total).astype(jnp.bfloat16), top, total

    def give(b, body):
        def one(d):
            other = b * per_block + d

            @pl.when(other != me)
            def _():
                body(other)

        loop(per_block, one)

    for fetch in fetches[4:]:
        fetch.wait()
    drain(got_q.at[pl.ds(0, n - 1)], recvs.at[Q])
    drain(got_k.at[pl.ds(0, half - 1)], recvs.at[K])

    lane = lax.broadcasted_iota(jnp.int32, (q_block, 4 * rows), 1)
    diagonal = lane % rows == lax.broadcasted_iota(jnp.int32, (q_block, 4 * rows), 0) % rows

    head_of = lax.broadcasted_iota(jnp.int32, (folded.shape[0], inner), 1) // dim
    line = lax.broadcasted_iota(jnp.int32, (folded.shape[0], inner), 0)
    gains = 1.0 + modulation[1, pl.ds(place[3], 1), :]
    table = jnp.where(line == head_of, gains, jnp.where(line == heads, modulation[0, pl.ds(place[3], 1), :], 0.0))
    folded[...] = lax.dot_general(
        table,
        final_weight[...].astype(jnp.float32),
        transposed,
        precision=lax.Precision.HIGHEST,
        preferred_element_type=jnp.float32,
    )

    def image_block(i):
        b = (turn + i) % blocks
        devices = pl.ds(pl.multiple_of(b * per_block, per_block), per_block)
        stats = []
        for j in range(2):
            q = got_q[devices, :, j * dim : (j + 1) * dim].reshape(q_block, dim)
            at = 2 * j * dim
            k = got_k[:, :, at : at + dim].reshape(half * rows, dim)
            v = got_k[:, :, at + dim : at + 2 * dim].reshape(half * rows, dim)
            pick = slice(j * img_rows, (j + 1) * img_rows)
            ki = got_k[:, pick, 4 * dim : 5 * dim].reshape(half * img_rows, dim)
            vi = got_k[:, pick, 5 * dim :].reshape(half * img_rows, dim)
            o, top, total = attend(q, (k, ki), (v, vi))
            out_b[devices, :, j * dim : (j + 1) * dim] = o.reshape(per_block, rows, dim)
            stats += [top, total]
        x = jnp.where(lane < rows, stats[0], jnp.where(lane < 2 * rows, stats[1], jnp.where(lane < 3 * rows, stats[2], stats[3])))
        x = jnp.where(diagonal, x, 0.0).reshape(per_block, rows, 4 * rows)
        out_s[devices, 0, :] = jnp.sum(x, axis=1)

        def body(other):
            send(out_b.at[other], back_b.at[me], RB, other)
            send(out_s.at[other], back_s.at[me], RS, other)

        give(b, body)

    loop(blocks, image_block)
    back_b[me] = out_b[me]
    back_s[me] = out_s[me]

    spots = lax.broadcasted_iota(jnp.int32, (rows, 1), 0)

    def start_of(t, column):
        return jnp.where(spots == t, starts[frames[me * rows + t]], column)

    begin = lax.fori_loop(0, rows, start_of, jnp.zeros((rows, 1), jnp.int32))
    audio_rows = audio_kv.shape[0]
    audio_count = n * audio_rows
    slots = lax.broadcasted_iota(jnp.int32, (rows, audio_count), 1)
    inside = (slots >= begin) & (slots < begin + AUD_WIN)
    ranks = audio_q.shape[0]
    inside = jnp.concatenate([inside] * ranks, axis=0)

    drain(gathered.at[pl.ds(0, plane - 1)], recvs.at[NEAR])
    per = 8 // audio_rows

    def widen(g):
        pieces = []
        for i in range(per):
            src = g * per + i
            pieces.append(gathered[src % plane, src // plane].astype(jnp.float32))
        audio_wide[pl.ds(pl.multiple_of(g * 8, 8), 8), :] = jnp.concatenate(pieces, axis=0)

    loop(audio_count // 8, widen)
    def audio_head(h):
        cols = pl.ds(pl.multiple_of(h * dim, dim), dim)
        val_cols = pl.ds(pl.multiple_of(inner + h * dim, dim), dim)
        q = audio_q[:, :, cols].reshape(ranks * rows, dim)
        k = audio_wide[:, cols].astype(jnp.bfloat16)
        v = audio_wide[:, val_cols].astype(jnp.bfloat16)
        s = lax.dot_general(q, k, transposed, preferred_element_type=jnp.float32)
        s = jnp.where(inside, s, -jnp.inf)
        top = jnp.max(s, axis=1, keepdims=True)
        w = jnp.where(inside, jnp.exp2((s - top) * rate), 0.0)
        total = jnp.sum(w, axis=1, keepdims=True)
        o = jnp.dot(w.astype(jnp.bfloat16), v, preferred_element_type=jnp.float32) / total
        audio_out[:, :, cols] = o.reshape(ranks, rows, dim)

    loop(3 * heads // 4, audio_head)

    drain(got_c.at[pl.ds(0, n - 1)], recvs.at[C])

    def plain_block(i):
        b = (me // per_block + i) % blocks
        devices = pl.ds(pl.multiple_of(b * per_block, per_block), per_block)
        q = got_c[devices, :, 0:dim].reshape(q_block, dim)
        k = got_c[:, :, dim : 2 * dim].reshape(n * rows, dim)
        v = got_c[:, :, 2 * dim :].reshape(n * rows, dim)
        o, _, _ = attend(q, (k,), (v,))

        @pl.when(central)
        def _():
            out_c[devices] = o.reshape(per_block, rows, dim)
            give(b, lambda other: send(out_c.at[other], back_c.at[my_head], RC, other))

        @pl.when(jnp.logical_not(central))
        def _():
            x = o.astype(jnp.float32)
            center = jnp.mean(x, axis=1, keepdims=True)
            x = x - center
            spread = jnp.sum(jnp.square(x), axis=1, keepdims=True)
            cols = pl.ds(pl.multiple_of(my_head * dim, dim), dim)
            chosen = lax.broadcasted_iota(jnp.int32, (branches, dim), 0) == place[3]
            gain = jnp.sum(jnp.where(chosen, modulation[1, :, cols], 0.0), axis=0, keepdims=True)
            x = (x * (1.0 + gain)).astype(jnp.bfloat16)
            y = lax.dot_general(x, final_weight[:, cols], transposed, preferred_element_type=jnp.float32)
            y = y.reshape(per_block, rows, channels)
            y = jnp.concatenate([y[:, : rows // 2], y[:, rows // 2 :]], axis=2)
            out_y[devices] = y.astype(jnp.bfloat16)
            z = jnp.where(lane < rows, center, jnp.where(lane < 2 * rows, spread, 0.0))
            z = jnp.where(diagonal, z, 0.0).reshape(per_block, rows, 4 * rows)
            out_z[devices, 0, :] = jnp.sum(z, axis=1)

            def body(other):
                send(out_y.at[other], back_y.at[my_head], RY, other)
                send(out_z.at[other], back_z.at[my_head], RZ, other)

            give(b, body)

    loop(blocks, plain_block)

    @pl.when(central)
    def _():
        back_c[my_head] = out_c[me]

    @pl.when(jnp.logical_not(central))
    def _():
        back_y[my_head] = out_y[me]
        back_z[my_head] = out_z[me]

    loop(heads - 3 * heads // 4, lambda i: audio_head(3 * heads // 4 + i))
    swapped = jnp.where(place[0] > place[1], 1, 0)
    seats = (swapped, 1 - swapped)

    def finish(p, result):
        x = hidden[...]
        center = jnp.mean(x, axis=1, keepdims=True)
        x = x - center
        spread = jnp.mean(jnp.square(x), axis=1, keepdims=True)
        x = x * lax.rsqrt(spread + 1e-06)
        gain = modulation[1, pl.ds(place[p], 1), :]
        shift = modulation[0, pl.ds(place[p], 1), :]
        x = (x * (1.0 + gain) + shift).astype(jnp.bfloat16)
        y = lax.dot_general(x, final_weight[...], transposed, preferred_element_type=jnp.float32)
        return result + guide[place[p]].astype(jnp.float32) * y

    result = jnp.zeros(mixed.shape, jnp.float32)
    drain(back_b.at[pl.ds(0, n - 1)], recvs.at[RB])
    drain(back_s.at[pl.ds(0, n - 1)], recvs.at[RS])
    a, b = back_s[0:half, 0, :], back_s[half:n, 0, :]
    most = jnp.maximum(a, b)
    lanes = 4 * rows
    a = jnp.exp2((a - most) * rate) * pltpu.roll(a, lanes - rows, 1)
    b = jnp.exp2((b - most) * rate) * pltpu.roll(b, lanes - rows, 1)
    whole = a + b
    parts = [a / whole, b / whole, jnp.zeros((lanes - n, lanes), jnp.float32)]
    weights[...] = jnp.concatenate(parts, axis=0).T
    for j in range(2):
        p = 2 * j
        tokens = slice(2 * j * rows, (2 * j + 1) * rows)
        for h in range(heads):
            cols = slice(h * dim, (h + 1) * dim)
            x = weights[tokens, h : h + 1] * back_b[h, :, j * dim : (j + 1) * dim].astype(jnp.float32)
            other = half + h
            x = x + weights[tokens, other : other + 1] * back_b[other, :, j * dim : (j + 1) * dim].astype(jnp.float32)
            if PAIRS[p][0]:
                x = x + audio_out[seats[p], :, cols]
            hidden[:, cols] = x
        result = finish(p, result)

    @pl.when(central)
    def _():
        drain(back_y, recvs.at[RY])
        drain(back_z, recvs.at[RZ])

    @pl.when(jnp.logical_not(central))
    def _():
        drain(back_y.at[pl.ds(0, heads - 1)], recvs.at[RY])
        drain(back_z.at[pl.ds(0, heads - 1)], recvs.at[RZ])

    z = back_z[:, 0, :]
    center = jnp.mean(z, axis=0, keepdims=True)
    away = z - center
    spread = jnp.sum(pltpu.roll(z, lanes - rows, 1) + dim * jnp.square(away), axis=0, keepdims=True) / inner
    parts = [away, lax.rsqrt(spread + 1e-06), jnp.zeros((lanes - heads - 1, lanes), jnp.float32)]
    weights[...] = jnp.concatenate(parts, axis=0).T
    y = functools.reduce(jnp.add, [back_y[h].astype(jnp.float32) for h in range(heads)])
    y = jnp.concatenate([y[:, :channels], y[:, channels:]], axis=0)
    for h in range(heads):
        y = y + weights[0:rows, h : h + 1] * folded[h : h + 1, :]
    y = weights[0:rows, heads : heads + 1] * y + folded[heads : heads + 1, :]
    result = result + guide[place[3]].astype(jnp.float32) * y

    @pl.when(central)
    def _():
        drain(back_c.at[pl.ds(0, heads - 1)], recvs.at[RC])

    @pl.when(jnp.logical_not(central))
    def _():
        drain(back_c, recvs.at[RC])

    for h in range(heads):
        cols = slice(h * dim, (h + 1) * dim)
        hidden[:, cols] = back_c[h].astype(jnp.float32) + audio_out[seats[1], :, cols]
    result = finish(1, result)
    mixed[...] = result

    drain(gathered.at[0, pl.ds(0, strips - 1)], sends.at[FAR])
    drain(gathered.at[pl.ds(0, plane - 1)], sends.at[NEAR])
    drain(got_q.at[pl.ds(0, n - 1)], sends.at[Q])
    drain(got_k.at[pl.ds(0, half - 1)], sends.at[K])
    drain(got_c.at[pl.ds(0, n - 1)], sends.at[C])
    drain(back_b.at[pl.ds(0, n - 1)], sends.at[RB])
    drain(back_s.at[pl.ds(0, n - 1)], sends.at[RS])

    @pl.when(central)
    def _():
        drain(out_c.at[pl.ds(0, n - 1)], sends.at[RC])

    @pl.when(jnp.logical_not(central))
    def _():
        drain(out_y.at[pl.ds(0, n - 1)], sends.at[RY])
        drain(out_z.at[pl.ds(0, n - 1)], sends.at[RZ])


def shards(
    video_heads,
    image_heads,
    audio_queries,
    audio_keys,
    condition_flags,
    guidance_weights,
    token_frame,
    window_start,
    modulation,
    final_weight,
    noisy_latent,
):
    heads, branches, rows, wide = video_heads.shape
    dim = wide // 3
    img_rows = image_heads.shape[2]
    n = lax.axis_size("seq")
    units = heads * branches // n
    assert n & (n - 1) == 0 and units in (1, 2, 4)
    bits = (n - 1).bit_length()
    plane = 2 ** ((bits + 1) // 2)
    tokens = n * rows
    q_block = min(256, tokens)
    images = max(1, units // 2)
    inner = heads * dim
    bf16, f32 = jnp.bfloat16, jnp.float32
    dma = pltpu.SemaphoreType.DMA
    def like(x, space):
        return space(x.shape, x.dtype)

    columns = final_weight.T
    small = (condition_flags, guidance_weights, token_frame, window_start)
    large = (video_heads, image_heads, audio_queries, audio_keys, modulation, columns)
    channels = final_weight.shape[1]
    if 2 * heads == n and branches == 4 and 4 * rows == 128 and rows == 2 * img_rows and channels == 64:
        half = n // 2
        kernel = split_kernel
        working = [
            pltpu.VMEM((heads, rows, 2 * dim), bf16),
            pltpu.VMEM((heads, rows, 6 * dim), bf16),
            pltpu.VMEM((n, rows, wide), bf16),
            pltpu.VMEM((n, rows, 2 * dim), bf16),
            pltpu.VMEM((half, rows, 6 * dim), bf16),
            pltpu.VMEM((n, rows, wide), bf16),
            pltpu.VMEM((n, rows, 2 * dim), bf16),
            pltpu.VMEM((n, 1, 4 * rows), f32),
            pltpu.VMEM((n, rows, dim), bf16),
            pltpu.VMEM((n, rows // 2, 2 * channels), bf16),
            pltpu.VMEM((n, 1, 4 * rows), f32),
            pltpu.VMEM((n, rows, 2 * dim), bf16),
            pltpu.VMEM((n, 1, 4 * rows), f32),
            pltpu.VMEM((heads, rows, dim), bf16),
            pltpu.VMEM((heads, rows // 2, 2 * channels), bf16),
            pltpu.VMEM((heads, 1, 4 * rows), f32),
            pltpu.VMEM((plane, n // plane) + audio_keys.shape, bf16),
            pltpu.VMEM((n * audio_keys.shape[0], 2 * inner), f32),
            pltpu.VMEM((audio_queries.shape[0], rows, inner), f32),
            pltpu.VMEM((rows, inner), f32),
            pltpu.VMEM((4 * rows, 4 * rows), f32),
            pltpu.VMEM((-(-(heads + 1) // 8) * 8, channels), f32),
            dma((10,)),
            dma((10,)),
            pltpu.SemaphoreType.REGULAR,
        ]
    else:
        kernel = step_kernel
        working = [
            pltpu.VMEM((heads * branches, rows, wide), bf16),
            pltpu.VMEM((heads * branches // 2, img_rows, 2 * dim), bf16),
            pltpu.VMEM((units, tokens, wide), bf16),
            pltpu.VMEM((images, n * img_rows, 2 * dim), bf16),
            pltpu.VMEM((units, tokens, dim), bf16),
            pltpu.VMEM((units, n, rows, dim), bf16),
            pltpu.VMEM((plane, n // plane) + audio_keys.shape, bf16),
            pltpu.VMEM((n * audio_keys.shape[0], 2 * inner), f32),
            pltpu.VMEM((audio_queries.shape[0], rows, inner), f32),
            pltpu.VMEM((rows, inner), f32),
            dma((units,)),
            dma((units,)),
            dma((images,)),
            dma((images,)),
            dma,
            dma,
            dma,
            dma,
            dma((units,)),
            dma((units,)),
        ]
    mixed = pl.pallas_call(
        functools.partial(kernel, n, q_block, plane),
        out_shape=jax.ShapeDtypeStruct(noisy_latent.shape, f32),
        in_specs=[pl.BlockSpec(memory_space=pl.ANY)] * (len(small) + len(large)),
        out_specs=pl.BlockSpec(memory_space=pltpu.VMEM),
        scratch_shapes=[
            *[like(x, pltpu.SMEM) for x in small],
            *[like(x, pltpu.VMEM) for x in large],
            dma((len(small) + len(large),)),
            *working,
        ],
        compiler_params=pltpu.CompilerParams(
            collective_id=0, has_side_effects=True, vmem_limit_bytes=67026944
        ),
        name="avatar_step",
    )(*small, *large)
    velocity = mixed / 8.0
    return (velocity, noisy_latent - 0.125 * velocity)


def solution(mesh):
    in_specs = (
        P("groups", None, "seq", None),
        P("groups", None, "seq", None),
        P("groups", "seq", None),
        P("seq", "groups"),
        P("groups", None),
        P("groups"),
        P("groups"),
        P("groups"),
        P("groups", None, None),
        P(),
        P(("groups", "seq"), None),
    )
    out_specs = (P(("groups", "seq"), None), P(("groups", "seq"), None))
    return jax.shard_map(shards, mesh=mesh, in_specs=in_specs, out_specs=out_specs, check_vma=False)
```
